1024 devices in a mesh: dp: 128 (over z, y_hi, core), mp: 8 (over x, y_lo).
Axes of the slice: x: 4, y: 4 (y_hi: 2, y_lo: 2; y = y_hi * 2 + y_lo), z: 32, core: 2. Of those that a mesh axis runs over, the one named last changes fastest.
Arguments:
- frames: bfloat16 [24576, 1536], P('dp', 'mp'), may hold values from -24 to 24
- frame_owner: int32 [24576, 1], P('dp'), may hold values from 0 to 127; in each aligned block of 192 rows (0 to 191, 192 to 383, ...) at most 2 rows name the same one
- frame_valid: int32 [24576], P('dp'), may hold values 0 or 1
- norm_gain: float32 [1536], replicated, may hold values from 0.1 to 1.9
- value_weight: bfloat16 [1536, 1536], P('dp', 'mp'), may hold values from -0.15625 to 0.15625
- gate_weight: bfloat16 [1536, 1536], P('dp', 'mp'), may hold values from -0.15625 to 0.15625
- grad_owned: bfloat16 [128, 128, 2, 1536], P('dp', None, None, 'mp'), may hold values from -6 to 6
Outputs:
- gated_owned: bfloat16 [128, 128, 2, 1536], P('dp', None, None, 'mp')
- value_grad: float32 [1536, 1536], P('dp', 'mp')
- gate_grad: float32 [1536, 1536], P('dp', 'mp')
- normed_grad: bfloat16 [128, 128, 2, 1536], P('dp', None, None, 'mp')
The draws below stay inside these ranges and needn't reach their ends.
Inputs may be any that keep to these rules, and one draw needn't show every extreme that they name: `frame_owner`: within the rows of one device (aligned blocks of 192 rows) no owner is named more than 2 times, a bound that some block reaches.
All inputs are finite; a program needn't handle non-finite values. No bound on the sum of `frame_valid` on one device may be relied on, other than what follows from the above.
Results may differ from the reference program's by a relative error of at most 0.013.
Values may be sent and summed in bfloat16 or wider, within the bound.
No kernel may reach another device: no remote copies, remote signals or barrier semaphores. Data moves between devices by JAX's collectives and lax.ppermute only.
A program may use at most 32 MiB of HBM per device.

```python
import math
import jax
import jax.numpy as jnp
import numpy as np
from jax import lax

D = 1536
ROWS_DEV = 192
TOKENS = 24576
CAP = 2
N_DP = 128
N_MP = 8


def touch_ends(entries, rng, smallest, high):
    longest = entries.shape.index(max(entries.shape))
    spots = []
    for shift in (0, 1):
        where = [jax.random.randint(jax.random.fold_in(rng, axis), (), 0, length) for axis, length in enumerate(entries.shape)]
        where[longest] = (where[longest] + shift) % entries.shape[longest]
        spots.append(tuple(where))
    return entries.at[spots[0]].set(smallest).at[spots[1]].set(high)


def raised(result, own_key, source, target, shards_of, factor):
    def block_of(position):
        return (jnp.arange(result.shape[position]) // (result.shape[position] // shards_of)).reshape((-1,) + (1,) * (result.ndim - 1 - position))

    one_side = jax.random.permutation(own_key, shards_of)[block_of(target)]
    far = (block_of(target) + shards_of // 2) % shards_of
    return jnp.where((block_of(source) == one_side) | (block_of(source) == far), factor * result, result)


def block_scale(key, dims, cuts, smallest, high):
    def one(dim, parts):
        draws = jax.random.uniform(jax.random.fold_in(jax.random.fold_in(key, 6), dim), (parts,), jnp.float32, smallest / len(cuts), high / len(cuts))
        return jnp.repeat(jnp.exp(draws), dims[dim] // parts).reshape((-1,) + (1,) * (len(dims) - dim - 1))

    gain = one(*cuts[0])
    for cut in cuts[1:]:
        gain = gain * one(*cut)
    return gain


def routed_block(key, own, number, rows, count, top, limit, lean):
    ranking = jax.random.permutation(key, count)
    crowded, usual = portions_of(count, rows * top, limit, lean, True), portions_of(count, rows * top, limit, lean, False)
    places = jnp.arange(count)

    def named(lengths, turn):
        used = int((lengths > 0).sum())
        fixed = max(1, used // 4)
        moved = fixed + (places - fixed + turn * (used - fixed)) % max(1, count - fixed)
        return jnp.zeros((count,), jnp.int32).at[ranking[jnp.where(places < fixed, places, moved)]].set(jnp.asarray(lengths, jnp.int32))

    lengths = jnp.where(number % 4 == 0, named(crowded, number // 4), named(usual, number - number // 4 - 1))
    mixed = jax.random.permutation(jax.random.fold_in(own, 3), count)
    donor, receiver = mixed[0:count // 2 * 2:2], mixed[1:count // 2 * 2:2]
    slack = jnp.minimum(lengths[donor] - 1, limit - lengths[receiver]) // 2
    slack = jnp.where((donor == ranking[0]) | (receiver == ranking[0]) | (lengths[receiver] == 0), 0, jnp.maximum(slack, 0))
    moved = jax.random.randint(jax.random.fold_in(own, 4), (count // 2,), 0, 1 << 20) % (slack + 1)
    lengths = lengths.at[donor].add(-moved).at[receiver].add(moved)
    labels = jnp.searchsorted(jnp.cumsum(lengths), jnp.arange(rows * top), side="right").astype(jnp.int32)
    table = labels.reshape(top, rows).T
    table = table[jax.random.permutation(jax.random.fold_in(own, 1), rows)]
    turn = jax.random.randint(jax.random.fold_in(own, 2), (rows, 1), 0, top)
    return jnp.take_along_axis(table, (jnp.arange(top)[None, :] + turn) % top, axis=1)


def portions_of(number_of, total, limit, lean, full):
    portions = [(1 << 20) // math.isqrt(grade ** lean) + 1 for grade in range(1, number_of + 1)]
    largest = limit if full else min(limit, max(-(-total // number_of), total * portions[0] // sum(portions)))
    least = 1 if total - largest >= number_of - 1 else 0
    given, rest = [largest] + [least] * (number_of - 1), total - largest - least * (number_of - 1)
    while rest > 0:
        free = [i for i in range(1, number_of) if given[i] < largest] or [i for i in range(1, number_of) if given[i] < limit]
        mass, remaining = sum([portions[i] for i in free]), rest
        for i in free:
            more = min(limit - given[i], max(1, remaining * portions[i] // mass), rest)
            given[i] = given[i] + more
            rest = rest - more
    return np.array(given)


def gaussian(rng, extent, width, limit, split=(), held_as=jnp.bfloat16):
    drawn = jax.random.normal(rng, extent, jnp.float32) * width
    if len(split) > 0:
        drawn = block_scale(rng, extent, split, -0.22, 0.18) * drawn
    return jnp.clip(drawn, min=-limit, max=limit).astype(held_as)


def gaussian_with(own_key, shape, deviation, bound, shards, heavy, held_as=jnp.bfloat16):
    drawn = deviation * jax.random.normal(own_key, shape, jnp.float32)
    if shards:
        drawn = drawn * block_scale(own_key, shape, shards, -0.22, 0.18)
    return jnp.clip(raised(drawn, jax.random.fold_in(own_key, 3), *heavy), -bound, bound).astype(held_as)


def setup_inputs(seed: int = 0) -> dict:
    key_list = jax.random.split(jax.random.key(seed), 8)
    frames = gaussian_with(key_list[0], (TOKENS, D), 1.0, 24.0, ((0, 128), (1, 8)), (0, 1, 128, 5.5))
    frame_owner_keys = jax.random.split(jax.random.fold_in(key_list[1], 1), TOKENS // ROWS_DEV)
    frame_owner_turns = jax.random.permutation(jax.random.fold_in(key_list[1], 3), TOKENS // ROWS_DEV)
    frame_owner = jax.vmap(lambda own, number: routed_block(jax.random.fold_in(key_list[1], 2), own, number, ROWS_DEV, N_DP, 1, CAP, 2))(frame_owner_keys, frame_owner_turns).reshape((TOKENS, 1))
    frame_valid = touch_ends((jax.random.randint(key_list[2], (TOKENS,), 0, 8) < 7).astype(jnp.int32), jax.random.fold_in(key_list[2], 1), 0, 1)
    norm_gain = jnp.clip(1.0 + 0.18 * jax.random.normal(key_list[3], (D,), jnp.float32), 0.1, 1.9)
    value_weight = gaussian(key_list[4], (D, D), D ** -0.5, 0.15625, ((0, 128), (1, 8)))
    gate_weight = gaussian(key_list[5], (D, D), D ** -0.5, 0.15625, ((0, 128), (1, 8)))
    grad_owned = gaussian(key_list[6], (N_DP, N_DP, CAP, D), 1.0, 6.0, ((0, 128), (3, 8)))
    return {"frames": frames, "frame_owner": frame_owner, "frame_valid": frame_valid, "norm_gain": norm_gain, "value_weight": value_weight, "gate_weight": gate_weight, "grad_owned": grad_owned}


epsilon = 1e-05

def reference(frames, frame_owner, frame_valid, norm_gain, value_weight, gate_weight, grad_owned):
    owners = frame_owner.reshape(N_DP, ROWS_DEV).astype(jnp.int32)
    positions = jnp.arange(ROWS_DEV, dtype=jnp.int32)
    earlier = positions[None, :] < positions[:, None]
    same_owner = owners[:, :, None] == owners[:, None, :]
    slot_index = lax.optimization_barrier(jnp.sum((same_owner & earlier[None]).astype(jnp.int32), axis=2))
    sources = jnp.arange(N_DP, dtype=jnp.int32)[:, None]
    targets = ((owners * N_DP + sources) * CAP + slot_index).reshape(-1).astype(jnp.int32)
    slot_total = N_DP * N_DP * CAP
    placed = jnp.zeros((slot_total, D), jnp.bfloat16).at[targets].set(frames)
    live_flags = jnp.zeros((slot_total,), jnp.float32).at[targets].set(frame_valid.astype(jnp.float32))
    wide = placed.astype(jnp.float32)
    row_mean = lax.optimization_barrier(jnp.mean(wide, axis=1, keepdims=True))
    centred = wide - row_mean
    row_var = lax.optimization_barrier(jnp.mean(centred * centred, axis=1, keepdims=True))
    normed = (centred * lax.rsqrt(row_var + epsilon) * norm_gain * live_flags[:, None]).astype(jnp.bfloat16)
    value_act = jnp.dot(normed, value_weight, preferred_element_type=jnp.float32)
    gate_act = jnp.dot(normed, gate_weight, preferred_element_type=jnp.float32)
    gate_sig = jax.nn.sigmoid(gate_act)
    gated = (value_act * gate_sig).astype(jnp.bfloat16)
    upstream = grad_owned.reshape(slot_total, D).astype(jnp.float32)
    live_col = live_flags[:, None]
    value_delta = (upstream * gate_sig * live_col).astype(jnp.bfloat16)
    gate_delta = (upstream * value_act * gate_sig * (1.0 - gate_sig) * live_col).astype(jnp.bfloat16)
    scale = float(TOKENS) ** (-0.5)
    value_grad = jnp.dot(normed.T, value_delta, preferred_element_type=jnp.float32) * scale
    gate_grad = jnp.dot(normed.T, gate_delta, preferred_element_type=jnp.float32) * scale
    group_width = D // N_MP
    input_grad = jnp.zeros((slot_total, D), jnp.float32)
    for group in range(N_MP):
        first = group * group_width
        last = first + group_width
        partial_term = jnp.dot(value_delta[:, first:last], value_weight[:, first:last].T, preferred_element_type=jnp.float32) + jnp.dot(gate_delta[:, first:last], gate_weight[:, first:last].T, preferred_element_type=jnp.float32)
        input_grad = input_grad + partial_term.astype(jnp.bfloat16).astype(jnp.float32)
    shape_out = (N_DP, N_DP, CAP, D)
    return (gated.reshape(shape_out), value_grad, gate_grad, input_grad.astype(jnp.bfloat16).reshape(shape_out))
```

```python
import jax
import jax.numpy as jnp
from jax import lax
from jax.experimental import pallas as pl
from jax.experimental.pallas import tpu as pltpu
from jax.sharding import Mesh, PartitionSpec as P

epsilon = 1e-05
bf16, f32, i32 = jnp.bfloat16, jnp.float32, jnp.int32
YC = ("yh", "co")
DP = ("z", "yh", "co")
MP = ("x", "yl")
INTERPRET = False


def nt(a, b):
    return lax.dot_general(a, b, (((1,), (1,)), ((), ())), preferred_element_type=f32)


def nn(a, b):
    return lax.dot_general(a, b, (((1,), (0,)), ((), ())), preferred_element_type=f32)


def tn(a, b):
    return lax.dot_general(a, b, (((0,), (0,)), ((), ())), preferred_element_type=f32)


def call(kernel, outs, *args, scratch=()):
    vmem = pl.BlockSpec(memory_space=pltpu.VMEM)
    return pl.pallas_call(
        kernel,
        in_specs=[vmem] * len(args),
        out_specs=[vmem] * len(outs),
        out_shape=[jax.ShapeDtypeStruct(s, d) for s, d in outs],
        scratch_shapes=list(scratch),
        interpret=INTERPRET,
    )(*args)


def natural_of(p):
    return ((p // 12) % 4) * 48 + (p // 48) * 12 + p % 12


def turn_kernel(rows_ref, out_ref, live_ref, *, width, peers):
    slots = 2 * peers
    lanes = rows_ref.shape[1]
    rows = rows_ref[...]
    place = lax.broadcasted_iota(i32, (width, lanes), 0)
    column = lax.broadcasted_iota(i32, (width, lanes), 1)
    pick = (column == natural_of(place)).astype(bf16)
    flag = (lax.broadcasted_iota(i32, (16, lanes), 1) == width).astype(bf16)
    source = lax.broadcasted_iota(i32, (slots, slots), 0)
    target = lax.broadcasted_iota(i32, (slots, slots), 1)
    order = (source == (target % peers) * 2 + target // peers).astype(bf16)
    turned = nt(jnp.concatenate([pick, flag], axis=0), rows).astype(bf16)
    ordered = nn(turned, order)
    out_ref[...] = ordered[:width].astype(bf16)
    live_ref[...] = ordered[width : width + 8]


def main_kernel(whole_ref, live_ref, gain_ref, w_ref, up_ref, gated_ref, dw_ref, partial_ref, normed_ref):
    blocks, width, slots = whole_ref.shape
    peers = slots // 2
    total = blocks * width
    live = live_ref[0:1, :]
    s = jnp.zeros((1, slots), f32)
    for m in range(blocks):
        s = s + jnp.sum(whole_ref[m].astype(f32), axis=0, keepdims=True)
    mean = s * (1.0 / total)
    s = jnp.zeros((1, slots), f32)
    for m in range(blocks):
        c = whole_ref[m].astype(f32) - mean
        s = s + jnp.sum(c * c, axis=0, keepdims=True)
    inv = lax.rsqrt(s * (1.0 / total) + epsilon)

    def w_block(m):
        return jnp.concatenate([w_ref[k, 48 * m : 48 * m + 48, :] for k in range(4)], axis=0)

    acc = jnp.zeros((2 * width, slots), f32)
    for m in range(blocks):
        c = whole_ref[m].astype(f32) - mean
        normed = (c * inv * gain_ref[m] * live).astype(bf16)
        normed_ref[m] = normed
        acc = acc + tn(w_block(m), normed)
    value, gate = acc[:width], acc[width:]
    sig = jax.nn.sigmoid(gate)
    up = jnp.concatenate([up_ref[0], up_ref[1]], axis=1).astype(f32)
    gated = (value * sig).astype(bf16)
    gated_ref[0] = gated[:, :peers]
    gated_ref[1] = gated[:, peers:]
    value_delta = (up * sig * live).astype(bf16)
    gate_delta = (up * value * sig * (1.0 - sig) * live).astype(bf16)
    delta = jnp.concatenate([value_delta, gate_delta], axis=0)
    for m in range(blocks):
        dw = nt(normed_ref[m], delta).astype(bf16)
        for k in range(4):
            dw_ref[k, 48 * m : 48 * m + 48, :] = dw[48 * k : 48 * k + 48]
        partial_ref[m] = nn(w_block(m), delta).astype(bf16)


def join_kernel(parts_ref, out_ref):
    blocks, width, slots = parts_ref.shape
    peers = slots // 2
    s = parts_ref[0].astype(f32)
    for m in range(1, blocks):
        s = s + parts_ref[m].astype(f32)
    place = lax.broadcasted_iota(i32, (width, width), 1)
    natural = lax.broadcasted_iota(i32, (width, width), 0)
    back = (natural_of(place) == natural).astype(bf16)
    out = nn(back, s.astype(bf16)).astype(bf16)
    out_ref[0] = out[:, :peers]
    out_ref[1] = out[:, peers:]


def spread(x, axis, count):
    return lax.all_to_all(jnp.broadcast_to(x[None], (count,) + x.shape), axis, 0, 0, tiled=True)


def body(frames, frame_owner, frame_valid, norm_gain, value_weight, gate_weight, grad_owned):
    z = lax.axis_size("z")
    blocks = lax.axis_size(MP)
    peers = 4 * z
    slots = 2 * peers
    rows, width = frames.shape
    group = value_weight.shape[0]
    lanes = -(-(width + 1) // 128) * 128

    shard = jnp.concatenate([value_weight, gate_weight], axis=1)
    w_z = spread(shard, "z", z)
    owner = frame_owner[:, 0]
    positions = jnp.arange(rows, dtype=i32)
    earlier = positions[None, :] < positions[:, None]
    same = owner[:, None] == owner[None, :]
    slot = jnp.sum((same & earlier).astype(i32), axis=1)
    targets = owner * 2 + slot
    placing = (jnp.arange(slots, dtype=i32)[:, None] == targets[None, :]).astype(bf16)
    flagged = jnp.concatenate(
        [frames, frame_valid.astype(bf16)[:, None], jnp.zeros((rows, lanes - width - 1), bf16)], axis=1
    )
    sent = jnp.dot(placing, flagged, preferred_element_type=f32).astype(bf16).reshape(peers, 2, lanes)
    got = lax.all_to_all(sent, DP, 0, 0, tiled=True).reshape(slots, lanes)
    turned, live = call(
        lambda *refs: turn_kernel(*refs, width=width, peers=peers),
        [((width, slots), bf16), ((8, slots), f32)],
        got,
    )
    whole = spread(turned, MP, blocks)
    w_full = spread(w_z.reshape(z * group, 2 * width), YC, 4)
    gain = norm_gain.reshape(blocks, 4, 4, 12).transpose(0, 2, 1, 3).reshape(blocks, width, 1)
    up = grad_owned.reshape(peers, 2, width).transpose(1, 2, 0)
    gated, dw, partial = call(
        main_kernel,
        [((2, width, peers), bf16), ((4, z * group, 2 * width), bf16), ((blocks, width, slots), bf16)],
        whole,
        live,
        gain,
        w_full,
        up,
        scratch=[pltpu.VMEM((blocks, width, slots), bf16)],
    )
    dw_yc = lax.all_to_all(dw, YC, 0, 0, tiled=True)
    dw_z = jnp.sum(dw_yc.astype(f32), axis=0).astype(bf16).reshape(z, group, 2 * width)
    dw_z = lax.all_to_all(dw_z, "z", 0, 0, tiled=True)
    parts = lax.all_to_all(partial, MP, 0, 0, tiled=True)
    (normed_grad,) = call(join_kernel, [((2, width, peers), bf16)], parts)
    scale = float(rows * peers) ** (-0.5)
    grads = jnp.sum(dw_z.astype(f32), axis=0) * scale

    def restore(x):
        return x.transpose(2, 0, 1).reshape(1, peers, 2, width)

    return (restore(gated), grads[:, :width], grads[:, width:], restore(normed_grad))


def solution(mesh):
    mp = mesh.shape["mp"]
    z = mesh.shape["dp"] // 4
    fine = Mesh(mesh.devices.reshape(z, 2, 2, mp // 2, 2), ("z", "yh", "co", "x", "yl"))
    slots = P(DP, None, None, MP)
    weights = P(DP, MP)
    return jax.shard_map(
        body,
        mesh=fine,
        in_specs=(P(DP, MP), P(DP, None), P(DP), P(), weights, weights, slots),
        out_specs=(slots, weights, weights, slots),
        check_vma=False,
    )
```

```python
import jax
import jax.numpy as jnp
from jax import lax
from jax.experimental import pallas as pl
from jax.experimental.pallas import tpu as pltpu
from jax.sharding import Mesh, PartitionSpec as P


epsilon = 1e-05
bf16, f32, i32 = jnp.bfloat16, jnp.float32, jnp.int32
YC = ("yh", "co")
DP = ("z", "yh", "co")
MP = ("x", "yl")
INTERPRET = False


def nt(a, b):
    return lax.dot_general(a, b, (((1,), (1,)), ((), ())), preferred_element_type=f32)


def nn(a, b):
    return lax.dot_general(a, b, (((1,), (0,)), ((), ())), preferred_element_type=f32)


def tn(a, b):
    return lax.dot_general(a, b, (((0,), (0,)), ((), ())), preferred_element_type=f32)


def call(kernel, outs, *args, limit=12):
    vmem = pl.BlockSpec(memory_space=pltpu.VMEM)
    smem = pl.BlockSpec(memory_space=pltpu.SMEM)
    return pl.pallas_call(
        kernel,
        in_specs=[smem if a.shape == (1,) else vmem for a in args],
        out_specs=[vmem] * len(outs),
        out_shape=[jax.ShapeDtypeStruct(s, d) for s, d in outs],
        compiler_params=pltpu.CompilerParams(vmem_limit_bytes=limit << 20),
        interpret=INTERPRET,
    )(*args)


def natural_of(p):
    return ((p // 12) % 4) * 48 + (p // 48) * 12 + p % 12


def turn_kernel(rows_ref, out_ref, live_ref, *, width, z):
    slots, lanes = rows_ref.shape
    peers = slots // 2
    rows = rows_ref[...]
    place = lax.broadcasted_iota(i32, (width, lanes), 0)
    column = lax.broadcasted_iota(i32, (width, lanes), 1)
    pick = (column == natural_of(place)).astype(bf16)
    flag = (lax.broadcasted_iota(i32, (16, lanes), 1) == width).astype(bf16)
    source = lax.broadcasted_iota(i32, (slots, slots), 0)
    target = lax.broadcasted_iota(i32, (slots, slots), 1)
    loader = target % peers
    order = (source == ((loader % 4) * z + loader // 4) * 2 + target // peers).astype(bf16)
    turned = nt(jnp.concatenate([pick, flag], axis=0), rows).astype(bf16)
    ordered = nn(turned, order)
    out_ref[...] = ordered[:width].astype(bf16)
    live_ref[...] = ordered[width : width + 8]


def block_of(own_ref, k, blocks):
    x, y = own_ref[0] // 2, own_ref[0] % 2
    return ((x + (blocks // 2 - k // 2)) % (blocks // 2)) * 2 + (y + k) % 2


def norm_kernel(own_ref, live_ref, gain_ref, *refs):
    normed_ref = refs[-1]
    blocks, width, slots = normed_ref.shape
    total = blocks * width
    live = live_ref[0:1, :]
    s = jnp.zeros((1, slots), f32)
    for k in range(blocks):
        s = s + jnp.sum(refs[k][...].astype(f32), axis=0, keepdims=True)
    mean = s * (1.0 / total)
    s = jnp.zeros((1, slots), f32)
    for k in range(blocks):
        c = refs[k][...].astype(f32) - mean
        s = s + jnp.sum(c * c, axis=0, keepdims=True)
    inv = lax.rsqrt(s * (1.0 / total) + epsilon)
    for k in range(blocks):
        c = refs[k][...].astype(f32) - mean
        normed_ref[k] = (c * inv * gain_ref[block_of(own_ref, k, blocks)] * live).astype(bf16)


def part_of(m):
    return pl.ds(pl.multiple_of(48 * m, 16), 48)


def w_block(w_ref, m):
    return jnp.concatenate([w_ref[j, part_of(m), :] for j in range(4)], axis=0)


def forward_kernel(own_ref, normed_ref, live_ref, w_ref, up_ref, gated_ref, dw_ref, delta_ref):
    blocks, width, slots = normed_ref.shape
    peers = slots // 2
    live = live_ref[0:1, :]
    acc = jnp.zeros((2 * width, slots), f32)
    for k in range(blocks):
        acc = acc + tn(w_block(w_ref, block_of(own_ref, k, blocks)), normed_ref[k])
    value, gate = acc[:width], acc[width:]
    sig = jax.nn.sigmoid(gate)
    up = jnp.concatenate([up_ref[0], up_ref[1]], axis=1).astype(f32)
    gated = (value * sig).astype(bf16)
    gated_ref[0] = gated[:, :peers]
    gated_ref[1] = gated[:, peers:]
    value_delta = (up * sig * live).astype(bf16)
    gate_delta = (up * value * sig * (1.0 - sig) * live).astype(bf16)
    delta = jnp.concatenate([value_delta, gate_delta], axis=0)
    delta_ref[...] = delta
    for k in range(blocks):
        dw = nt(normed_ref[k], delta).astype(bf16)
        m = block_of(own_ref, k, blocks)
        for j in range(4):
            dw_ref[j, part_of(m), :] = dw[48 * j : 48 * j + 48]


def backward_kernel(own_ref, w_ref, delta_ref, *partial_refs):
    blocks = len(partial_refs)
    for k in range(blocks):
        partial_refs[k][...] = nn(w_block(w_ref, block_of(own_ref, k, blocks)), delta_ref[...]).astype(bf16)


def join_kernel(*refs):
    out_ref = refs[-1]
    width, slots = refs[0].shape
    peers = slots // 2
    s = refs[0][...].astype(f32)
    for ref in refs[1:-1]:
        s = s + ref[...].astype(f32)
    place = lax.broadcasted_iota(i32, (width, width), 1)
    natural = lax.broadcasted_iota(i32, (width, width), 0)
    back = (natural_of(place) == natural).astype(bf16)
    out = nn(back, s.astype(bf16)).astype(bf16)
    out_ref[0] = out[:, :peers]
    out_ref[1] = out[:, peers:]


def spread(x, axis, count):
    return lax.all_to_all(jnp.broadcast_to(x[None], (count,) + x.shape), axis, 0, 0, tiled=True)


def hop(x, k, blocks, back):
    n = blocks // 2
    pairs = []
    for i in range(blocks):
        j = ((i // 2 + k // 2) % n) * 2 + (i % 2 + k) % 2
        pairs.append((j, i) if back else (i, j))
    return lax.ppermute(x, MP, pairs)


def tiles(x):
    return x.reshape(x.shape[0] // 4, 4, x.shape[1] // 128, 128).transpose(2, 0, 1, 3)


def body(frames, frame_owner, frame_valid, norm_gain, value_weight, gate_weight, grad_owned):
    z = lax.axis_size("z")
    blocks = lax.axis_size(MP)
    peers = 4 * z
    slots = 2 * peers
    rows, width = frames.shape
    group = value_weight.shape[0]
    columns = 2 * width
    wt = columns // 128 * group // 4
    lanes = -(-(width + 1) // 128) * 128
    halves = lanes // 128
    own = lax.axis_index(MP).astype(i32).reshape(1)

    shard = tiles(jnp.concatenate([value_weight, gate_weight], axis=1)).reshape(wt, 4, 128)
    owner = frame_owner[:, 0]
    positions = jnp.arange(rows, dtype=i32)
    earlier = positions[None, :] < positions[:, None]
    same = owner[:, None] == owner[None, :]
    slot = jnp.sum((same & earlier).astype(i32), axis=1)
    targets = owner * 2 + slot
    placing = (jnp.arange(slots, dtype=i32)[:, None] == targets[None, :]).astype(bf16)
    flagged = jnp.concatenate(
        [frames, frame_valid.astype(bf16)[:, None], jnp.zeros((rows, lanes - width - 1), bf16)], axis=1
    )
    sent = jnp.dot(placing, flagged, preferred_element_type=f32).astype(bf16)
    sent = sent.reshape(z, 2, 4, halves, 128).transpose(0, 3, 1, 2, 4).reshape(z, 2 * halves, 4, 128)
    sent = jnp.concatenate([jnp.broadcast_to(shard[None], (z,) + shard.shape), sent], axis=1)
    got = lax.all_to_all(sent, "z", 0, 0, tiled=True)
    rows_z = got[:, wt:].reshape(z, halves, 4, 2, 128).transpose(2, 0, 3, 1, 4).reshape(4, 2 * z, lanes)
    rows_y = lax.all_to_all(rows_z, YC, 0, 0, tiled=True)
    w_rows = got[:, :wt].reshape(z, columns // 128, group, 128).transpose(0, 2, 1, 3)
    w_rows = w_rows.reshape(z * group, columns)
    w_full = spread(w_rows, YC, 4)
    turned, live = call(
        lambda *refs: turn_kernel(*refs, width=width, z=z),
        [((width, slots), bf16), ((8, slots), f32)],
        rows_y.reshape(slots, lanes),
    )
    whole = [turned] + [hop(turned, k, blocks, False) for k in range(1, blocks)]
    gain = norm_gain.reshape(blocks, 4, 4, 12).transpose(0, 2, 1, 3).reshape(blocks, width, 1)
    (normed,) = call(norm_kernel, [((blocks, width, slots), bf16)], own, live, gain, *whole)
    up = grad_owned.reshape(peers, 2, width).transpose(1, 2, 0)
    gated, dw, delta = call(
        forward_kernel,
        [((2, width, peers), bf16), ((4, z * group, columns), bf16), ((columns, slots), bf16)],
        own,
        normed,
        live,
        w_full,
        up,
    )
    dw_y = lax.all_to_all(dw, YC, 0, 0, tiled=True)
    partial = call(backward_kernel, [((width, slots), bf16)] * blocks, own, w_full, delta)
    dw_y = jnp.sum(dw_y.astype(f32), axis=0).astype(bf16)
    dw_y = dw_y.reshape(z, group, columns // 128, 128).transpose(0, 2, 1, 3).reshape(z, wt, 4, 128)
    dw_z = lax.all_to_all(dw_y, "z", 0, 0, tiled=True)
    parts = [partial[0]] + [hop(partial[k], k, blocks, True) for k in range(1, blocks)]
    (normed_grad,) = call(join_kernel, [((2, width, peers), bf16)], *parts)
    scale = float(rows * peers) ** (-0.5)
    grads = jnp.sum(dw_z.astype(f32), axis=0) * scale
    grads = grads.reshape(columns // 128, group, 128).transpose(1, 0, 2).reshape(group, columns)

    def restore(x):
        return x.transpose(2, 0, 1).reshape(1, peers, 2, width)

    return (restore(gated), grads[:, :width], grads[:, width:], restore(normed_grad))


def solution(mesh):
    mp = mesh.shape["mp"]
    z = mesh.shape["dp"] // 4
    fine = Mesh(mesh.devices.reshape(z, 2, 2, mp // 2, 2), ("z", "yh", "co", "x", "yl"))
    slots = P(DP, None, None, MP)
    weights = P(DP, MP)
    return jax.shard_map(
        body,
        mesh=fine,
        in_specs=(P(DP, MP), P(DP, None), P(DP), P(), weights, weights, slots),
        out_specs=(slots, weights, weights, slots),
        check_vma=False,
    )
```

```python
import jax
import jax.numpy as jnp
from jax import lax
from jax.experimental import pallas as pl
from jax.experimental.pallas import tpu as pltpu
from jax.sharding import Mesh, PartitionSpec as P


epsilon = 1e-05
bf16, f32, i32 = jnp.bfloat16, jnp.float32, jnp.int32
NEAR = ("zl", "yh", "co")
DP = ("zh", "zl", "yh", "co")
MP = ("x", "yl")
INTERPRET = False


def nt(a, b):
    return lax.dot_general(a, b, (((1,), (1,)), ((), ())), preferred_element_type=f32)


def nn(a, b):
    return lax.dot_general(a, b, (((1,), (0,)), ((), ())), preferred_element_type=f32)


def tn(a, b):
    return lax.dot_general(a, b, (((0,), (0,)), ((), ())), preferred_element_type=f32)


def call(kernel, outs, *args, limit=12):
    vmem = pl.BlockSpec(memory_space=pltpu.VMEM)
    smem = pl.BlockSpec(memory_space=pltpu.SMEM)
    return pl.pallas_call(
        kernel,
        in_specs=[smem if a.shape == (1,) else vmem for a in args],
        out_specs=[vmem] * len(outs),
        out_shape=[jax.ShapeDtypeStruct(s, d) for s, d in outs],
        compiler_params=pltpu.CompilerParams(vmem_limit_bytes=limit << 20),
        interpret=INTERPRET,
    )(*args)


def natural_of(p):
    return ((p // 12) % 2) * 96 + (p // 24) * 12 + p % 12


def turn_kernel(rows_ref, out_ref, live_ref, *, width, far):
    slots, lanes = rows_ref.shape
    peers = slots // 2
    rows = rows_ref[...]
    place = lax.broadcasted_iota(i32, (width, lanes), 0)
    column = lax.broadcasted_iota(i32, (width, lanes), 1)
    pick = (column == natural_of(place)).astype(bf16)
    flag = (lax.broadcasted_iota(i32, (16, lanes), 1) == width).astype(bf16)
    source = lax.broadcasted_iota(i32, (slots, slots), 0)
    target = lax.broadcasted_iota(i32, (slots, slots), 1)
    loader = target % peers
    order = (source == ((loader % 8) * far + loader // 8) * 2 + target // peers).astype(bf16)
    turned = nt(jnp.concatenate([pick, flag], axis=0), rows).astype(bf16)
    ordered = nn(turned, order)
    out_ref[...] = ordered[:width].astype(bf16)
    live_ref[...] = ordered[width : width + 8]


def block_of(own_ref, k, blocks):
    x, y = own_ref[0] // 2, own_ref[0] % 2
    return ((x + (blocks // 2 - k // 2)) % (blocks // 2)) * 2 + (y + k) % 2


def norm_kernel(own_ref, live_ref, gain_ref, *refs):
    normed_ref = refs[-1]
    blocks, width, slots = normed_ref.shape
    total = blocks * width
    live = live_ref[0:1, :]
    s = jnp.zeros((1, slots), f32)
    for k in range(blocks):
        s = s + jnp.sum(refs[k // 2][k % 2].astype(f32), axis=0, keepdims=True)
    mean = s * (1.0 / total)
    s = jnp.zeros((1, slots), f32)
    for k in range(blocks):
        c = refs[k // 2][k % 2].astype(f32) - mean
        s = s + jnp.sum(c * c, axis=0, keepdims=True)
    inv = lax.rsqrt(s * (1.0 / total) + epsilon)
    for k in range(blocks):
        c = refs[k // 2][k % 2].astype(f32) - mean
        normed_ref[k] = (c * inv * gain_ref[block_of(own_ref, k, blocks)] * live).astype(bf16)


def w_block(w_ref, m):
    return jnp.concatenate([w_ref[j, m] for j in range(8)], axis=0)


def forward_kernel(own_ref, normed_ref, live_ref, w_ref, up_ref, gated_ref, dw_ref, delta_ref):
    blocks, width, slots = normed_ref.shape
    peers = slots // 2
    live = live_ref[0:1, :]
    acc = jnp.zeros((2 * width, slots), f32)
    for k in range(blocks):
        acc = acc + tn(w_block(w_ref, block_of(own_ref, k, blocks)), normed_ref[k])
    value, gate = acc[:width], acc[width:]
    sig = jax.nn.sigmoid(gate)
    up = jnp.concatenate([up_ref[0], up_ref[1]], axis=1).astype(f32)
    gated = (value * sig).astype(bf16)
    gated_ref[0] = gated[:, :peers]
    gated_ref[1] = gated[:, peers:]
    value_delta = (up * sig * live).astype(bf16)
    gate_delta = (up * value * sig * (1.0 - sig) * live).astype(bf16)
    delta = jnp.concatenate([value_delta, gate_delta], axis=0)
    delta_ref[...] = delta
    for k in range(blocks):
        dw = nt(normed_ref[k], delta)
        m = block_of(own_ref, k, blocks)
        for j in range(8):
            dw_ref[j, m] = dw[24 * j : 24 * j + 24].astype(bf16)


def backward_kernel(own_ref, w_ref, delta_ref, *partial_refs):
    blocks = 2 * len(partial_refs)
    for k in range(blocks):
        w = w_block(w_ref, block_of(own_ref, k, blocks))
        partial_refs[k // 2][k % 2] = nn(w, delta_ref[...]).astype(bf16)


def join_kernel(*refs):
    across_ref, out_ref = refs[-2:]
    width, slots = across_ref.shape[1:]
    peers = slots // 2
    s = jnp.zeros((width, slots), f32)
    for k, ref in enumerate(refs[:-2]):
        s = s + ref[0].astype(f32) + across_ref[k].astype(f32)
    place = lax.broadcasted_iota(i32, (width, width), 1)
    natural = lax.broadcasted_iota(i32, (width, width), 0)
    back = (natural_of(place) == natural).astype(bf16)
    out = nn(back, s.astype(bf16)).astype(bf16)
    out_ref[0] = out[:, :peers]
    out_ref[1] = out[:, peers:]


def spread(x, axis, count):
    return lax.all_to_all(jnp.broadcast_to(x[None], (count,) + x.shape), axis, 0, 0, tiled=True)


def hop(x, step):
    n = lax.axis_size("x")
    return lax.ppermute(x, "x", [(i, (i + step) % n) for i in range(n)])


def swap(x):
    return lax.ppermute(x, "yl", [(0, 1), (1, 0)])


def tiles(x):
    return x.reshape(x.shape[0] // 4, 4, x.shape[1] // 128, 128).transpose(2, 0, 1, 3)


def body(frames, frame_owner, frame_valid, norm_gain, value_weight, gate_weight, grad_owned):
    far = lax.axis_size("zh")
    blocks = lax.axis_size(MP)
    peers = 8 * far
    slots = 2 * peers
    rows, width = frames.shape
    group = value_weight.shape[0]
    columns = 2 * width
    wt = columns // 128 * group // 4
    lanes = -(-(width + 1) // 128) * 128
    halves = lanes // 128
    own = lax.axis_index(MP).astype(i32).reshape(1)

    shard = tiles(jnp.concatenate([value_weight, gate_weight], axis=1)).reshape(wt, 4, 128)
    owner = frame_owner[:, 0]
    positions = jnp.arange(rows, dtype=i32)
    earlier = positions[None, :] < positions[:, None]
    same = owner[:, None] == owner[None, :]
    slot = jnp.sum((same & earlier).astype(i32), axis=1)
    targets = owner * 2 + slot
    placing = (jnp.arange(slots, dtype=i32)[:, None] == targets[None, :]).astype(bf16)
    flagged = jnp.concatenate(
        [frames, frame_valid.astype(bf16)[:, None], jnp.zeros((rows, lanes - width - 1), bf16)], axis=1
    )
    sent = jnp.dot(placing, flagged, preferred_element_type=f32).astype(bf16)
    sent = sent.reshape(far, 4, 4, halves, 128).transpose(0, 3, 1, 2, 4).reshape(far, 4 * halves, 4, 128)
    sent = jnp.concatenate([jnp.broadcast_to(shard[None], (far,) + shard.shape), sent], axis=1)
    got = lax.all_to_all(sent, "zh", 0, 0, tiled=True)
    rows_z = got[:, wt:].reshape(far, halves, 8, 2, 128).transpose(2, 0, 3, 1, 4).reshape(8, 2 * far, lanes)
    rows_y = lax.all_to_all(rows_z, NEAR, 0, 0, tiled=True)
    w_rows = got[:, :wt].reshape(far, columns // 128, group, 128).transpose(0, 2, 1, 3)
    w_rows = w_rows.reshape(far * group, columns)
    w_full = spread(w_rows, NEAR, 8)
    w_full = w_full.reshape(8, blocks, 2 * group, columns)
    turned, live = call(
        lambda *refs: turn_kernel(*refs, width=width, far=far),
        [((width, slots), bf16), ((8, slots), f32)],
        rows_y.reshape(slots, lanes),
    )
    pair = jnp.stack([turned, swap(turned)])
    whole = [pair] + [hop(pair, dx) for dx in range(1, blocks // 2)]
    gain = norm_gain.reshape(blocks, 2, 8, 12).transpose(0, 2, 1, 3).reshape(blocks, width, 1)
    (normed,) = call(norm_kernel, [((blocks, width, slots), bf16)], own, live, gain, *whole)
    up = grad_owned.reshape(peers, 2, width).transpose(1, 2, 0)
    gated, dw, delta = call(
        forward_kernel,
        [((2, width, peers), bf16), ((8, blocks, 2 * group, columns), bf16), ((columns, slots), bf16)],
        own,
        normed,
        live,
        w_full,
        up,
    )
    dw_y = lax.all_to_all(dw.reshape(8, far * group, columns), NEAR, 0, 0, tiled=True)
    partial = call(backward_kernel, [((2, width, slots), bf16)] * (blocks // 2), own, w_full, delta)
    dw_y = jnp.sum(dw_y.astype(f32), axis=0).astype(bf16)
    dw_y = dw_y.reshape(far, group, columns // 128, 128).transpose(0, 2, 1, 3).reshape(far, wt, 4, 128)
    dw_z = lax.all_to_all(dw_y, "zh", 0, 0, tiled=True)
    parts = [partial[0]] + [hop(partial[dx], -dx) for dx in range(1, blocks // 2)]
    other = jnp.stack([p[1] for p in parts])
    across = swap(other)
    (normed_grad,) = call(join_kernel, [((2, width, peers), bf16)], *parts, across)
    scale = float(rows * peers) ** (-0.5)
    grads = jnp.sum(dw_z.astype(f32), axis=0) * scale
    grads = grads.reshape(columns // 128, group, 128).transpose(1, 0, 2).reshape(group, columns)

    def restore(x):
        return x.transpose(2, 0, 1).reshape(1, peers, 2, width)

    return (restore(gated), grads[:, :width], grads[:, width:], restore(normed_grad))


def solution(mesh):
    mp = mesh.shape["mp"]
    far = mesh.shape["dp"] // 8
    fine = Mesh(mesh.devices.reshape(far, 2, 2, 2, mp // 2, 2), DP + MP)
    slots = P(DP, None, None, MP)
    weights = P(DP, MP)
    return jax.shard_map(
        body,
        mesh=fine,
        in_specs=(P(DP, MP), P(DP, None), P(DP), P(), weights, weights, slots),
        out_specs=(slots, weights, weights, slots),
        check_vma=False,
    )
```

```python
import jax
import jax.numpy as jnp
from jax import lax
from jax.experimental import pallas as pl
from jax.experimental.pallas import tpu as pltpu
from jax.sharding import Mesh, PartitionSpec as P


epsilon = 1e-05
bf16, f32, i32 = jnp.bfloat16, jnp.float32, jnp.int32
NEAR = ("zl", "yh")
DP = ("zh", "zl", "yh", "co")
MP = ("x", "yl")
INTERPRET = False


def nt(a, b):
    return lax.dot_general(a, b, (((1,), (1,)), ((), ())), preferred_element_type=f32)


def nn(a, b):
    return lax.dot_general(a, b, (((1,), (0,)), ((), ())), preferred_element_type=f32)


def tn(a, b):
    return lax.dot_general(a, b, (((0,), (0,)), ((), ())), preferred_element_type=f32)


def call(kernel, outs, *args, limit=12):
    vmem = pl.BlockSpec(memory_space=pltpu.VMEM)
    smem = pl.BlockSpec(memory_space=pltpu.SMEM)
    return pl.pallas_call(
        kernel,
        in_specs=[smem if a.shape == (2,) else vmem for a in args],
        out_specs=[vmem] * len(outs),
        out_shape=[jax.ShapeDtypeStruct(s, d) for s, d in outs],
        compiler_params=pltpu.CompilerParams(vmem_limit_bytes=limit << 20),
        interpret=INTERPRET,
    )(*args)


def natural_of(p, co):
    core = (p // 96 + co) % 2
    return ((p // 12) % 2) * 96 + (((p // 24) % 4) * 2 + core) * 12 + p % 12


def send_kernel(frames_ref, owner_ref, valid_ref, out_ref):
    rows, width = frames_ref.shape
    slots, lanes = out_ref.shape
    owner = owner_ref[...]
    down = jnp.transpose(jnp.broadcast_to(owner, (rows, rows)))
    earlier = lax.broadcasted_iota(i32, (rows, rows), 0) < lax.broadcasted_iota(i32, (rows, rows), 1)
    slot = jnp.sum(jnp.where((down == owner) & earlier, 1.0, 0.0), axis=0, keepdims=True).astype(i32)
    hit = lax.broadcasted_iota(i32, (slots, rows), 0) == owner * 2 + slot
    placed = nn(jnp.where(hit, 1.0, 0.0).astype(bf16), frames_ref[...])
    live = jnp.sum(jnp.where(hit & (valid_ref[...] > 0), 1.0, 0.0), axis=1, keepdims=True)
    pad = lax.broadcasted_iota(i32, (slots, lanes - width), 1) == 0
    out_ref[...] = jnp.concatenate([placed, jnp.where(pad, live, 0.0)], axis=1).astype(bf16)


def turn_kernel(own_ref, rows_ref, out_ref, live_ref):
    width, slots = out_ref.shape[1:]
    peers = slots // 2
    far = peers // 8
    lanes = rows_ref.shape[-1]
    place = lax.broadcasted_iota(i32, (width, lanes), 0)
    column = lax.broadcasted_iota(i32, (width, lanes), 1)
    pick = (column == natural_of(place, own_ref[1])).astype(bf16)
    flag = (lax.broadcasted_iota(i32, (16, lanes), 1) == width).astype(bf16)
    pick = jnp.concatenate([pick, flag], axis=0)
    source = lax.broadcasted_iota(i32, (slots, slots), 0)
    target = lax.broadcasted_iota(i32, (slots, slots), 1)
    loader = target % peers
    order = (source == ((loader % 8) * far + loader // 8) * 2 + target // peers).astype(bf16)
    for y in range(2):
        rows = jnp.concatenate([rows_ref[n, y] for n in range(8)], axis=0)
        ordered = nn(nt(pick, rows).astype(bf16), order)
        out_ref[y] = ordered[:width].astype(bf16)
    live_ref[...] = ordered[width : width + 8]


def block_of(own_ref, k, blocks, relative=False):
    x, y = own_ref[0] // 2, own_ref[0] % 2
    y = (y + k) % 2 if relative else k % 2
    return ((x + (blocks // 2 - k // 2)) % (blocks // 2)) * 2 + y


def norm_kernel(own_ref, live_ref, gain_ref, *refs):
    normed_ref = refs[-1]
    blocks, width, slots = normed_ref.shape
    total = blocks * width
    live = live_ref[0:1, :]
    s = jnp.zeros((1, slots), f32)
    for k in range(blocks):
        s = s + jnp.sum(refs[k // 2][k % 2].astype(f32), axis=0, keepdims=True)
    mean = s * (1.0 / total)
    s = jnp.zeros((1, slots), f32)
    for k in range(blocks):
        c = refs[k // 2][k % 2].astype(f32) - mean
        s = s + jnp.sum(c * c, axis=0, keepdims=True)
    inv = lax.rsqrt(s * (1.0 / total) + epsilon)
    for k in range(blocks):
        c = refs[k // 2][k % 2].astype(f32) - mean
        normed_ref[k] = (c * inv * gain_ref[block_of(own_ref, k, blocks)] * live).astype(bf16)


def w_block(wa_ref, wb_ref, m):
    return jnp.concatenate([ref[j, m] for ref in (wa_ref, wb_ref) for j in range(4)], axis=0)


def forward_kernel(own_ref, normed_ref, live_ref, wa_ref, wb_ref, up_ref, gated_ref, da_ref, db_ref, delta_ref):
    blocks, width, slots = normed_ref.shape
    peers = slots // 2
    live = live_ref[0:1, :]
    acc = jnp.zeros((2 * width, slots), f32)
    for k in range(blocks):
        acc = acc + tn(w_block(wa_ref, wb_ref, block_of(own_ref, k, blocks)), normed_ref[k])
    value, gate = acc[:width], acc[width:]
    sig = jax.nn.sigmoid(gate)
    up = jnp.concatenate([up_ref[0], up_ref[1]], axis=1).astype(f32)
    gated = (value * sig).astype(bf16)
    gated_ref[0] = gated[:, :peers]
    gated_ref[1] = gated[:, peers:]
    value_delta = (up * sig * live).astype(bf16)
    gate_delta = (up * value * sig * (1.0 - sig) * live).astype(bf16)
    delta = jnp.concatenate([value_delta, gate_delta], axis=0)
    delta_ref[...] = delta
    for k in range(blocks):
        dw = nt(normed_ref[k], delta)
        m = block_of(own_ref, k, blocks)
        for j in range(4):
            da_ref[j, m] = dw[24 * j : 24 * j + 24].astype(bf16)
            db_ref[j, m] = dw[24 * j + 96 : 24 * j + 120].astype(bf16)


def backward_kernel(own_ref, wa_ref, wb_ref, delta_ref, *partial_refs):
    blocks = 2 * len(partial_refs)
    for k in range(blocks):
        w = w_block(wa_ref, wb_ref, block_of(own_ref, k, blocks, True))
        partial_refs[k // 2][k % 2] = nn(w, delta_ref[...]).astype(bf16)


def join_kernel(own_ref, *refs):
    across_ref, out_ref = refs[-2:]
    width, slots = across_ref.shape[1:]
    peers = slots // 2
    s = jnp.zeros((width, slots), f32)
    for k, ref in enumerate(refs[:-2]):
        s = s + ref[0].astype(f32) + across_ref[k].astype(f32)
    place = lax.broadcasted_iota(i32, (width, width), 1)
    natural = lax.broadcasted_iota(i32, (width, width), 0)
    back = (natural_of(place, own_ref[1]) == natural).astype(bf16)
    out = nn(back, s.astype(bf16)).astype(bf16)
    out_ref[0] = out[:, :peers]
    out_ref[1] = out[:, peers:]


def spread(x, axis, count):
    return lax.all_to_all(jnp.broadcast_to(x[None], (count,) + x.shape), axis, 0, 0, tiled=True)


def hop(x, step):
    n = lax.axis_size("x")
    return lax.ppermute(x, "x", [(i, (i + step) % n) for i in range(n)])


def swap(x, axis):
    return lax.ppermute(x, axis, [(0, 1), (1, 0)])


def tiles(x):
    return x.reshape(x.shape[0] // 4, 4, x.shape[1] // 128, 128).transpose(2, 0, 1, 3)


def body(frames, frame_owner, frame_valid, norm_gain, value_weight, gate_weight, grad_owned):
    far = lax.axis_size("zh")
    blocks = lax.axis_size(MP)
    peers = 8 * far
    slots = 2 * peers
    rows, width = frames.shape
    group = value_weight.shape[0]
    columns = 2 * width
    wt = columns // 128 * group // 4
    lanes = -(-(width + 1) // 128) * 128
    halves = lanes // 128
    core = lax.axis_index("co").astype(i32)
    own = jnp.stack([lax.axis_index(MP).astype(i32), core])

    shard = tiles(jnp.concatenate([value_weight, gate_weight], axis=1)).reshape(wt, 4, 128)
    (sent,) = call(
        send_kernel, [((slots, lanes), bf16)], frames, frame_owner.reshape(1, rows), frame_valid.reshape(1, rows)
    )
    sent = sent.reshape(far, 4, 4, halves, 128).transpose(0, 3, 1, 2, 4).reshape(far, 4 * halves, 4, 128)
    sent = jnp.concatenate([jnp.broadcast_to(shard[None], (far,) + shard.shape), sent], axis=1)
    got = lax.all_to_all(sent, "zh", 0, 0, tiled=True)
    rows_z = got[:, wt:].reshape(far, halves, 8, 2, 128).transpose(2, 0, 3, 1, 4).reshape(8, 1, 2 * far, lanes)
    rows_z = jnp.broadcast_to(rows_z, (8, 2, 2 * far, lanes)).reshape(16, 2 * far, lanes)
    rows_y = lax.all_to_all(rows_z, ("zl", "yh", "co", "yl"), 0, 0, tiled=True)
    w_rows = got[:, :wt].reshape(far, columns // 128, group, 128).transpose(0, 2, 1, 3)
    w_rows = w_rows.reshape(far * group, columns)
    w_own = spread(w_rows, NEAR, 4)
    w_other = swap(w_own, "co")
    w_own = w_own.reshape(4, blocks, 2 * group, columns)
    w_other = w_other.reshape(4, blocks, 2 * group, columns)
    turned, live = call(
        turn_kernel,
        [((2, width, slots), bf16), ((8, slots), f32)],
        own,
        rows_y.reshape(8, 2, 2 * far, lanes),
    )
    whole = [turned] + [hop(turned, dx) for dx in range(1, blocks // 2)]
    gain = norm_gain.reshape(blocks, 2, 4, 2, 12).transpose(0, 3, 2, 1, 4)
    gain = jnp.where(core == 0, gain, gain[:, ::-1]).reshape(blocks, width, 1)
    (normed,) = call(norm_kernel, [((blocks, width, slots), bf16)], own, live, gain, *whole)
    up = grad_owned.reshape(peers, 2, width).transpose(1, 2, 0)
    near = (4, blocks, 2 * group, columns)
    gated, dw_own, dw_other, delta = call(
        forward_kernel,
        [((2, width, peers), bf16), (near, bf16), (near, bf16), ((columns, slots), bf16)],
        own,
        normed,
        live,
        w_own,
        w_other,
        up,
    )
    dw_c = swap(dw_other.reshape(4, far * group, columns), "co")
    partial = call(
        backward_kernel, [((2, width, slots), bf16)] * (blocks // 2), own, w_own, w_other, delta
    )
    dw_c = (dw_c.astype(f32) + dw_own.reshape(4, far * group, columns).astype(f32)).astype(bf16)
    dw_y = lax.all_to_all(dw_c, NEAR, 0, 0, tiled=True)
    dw_y = jnp.sum(dw_y.astype(f32), axis=0).astype(bf16)
    dw_y = dw_y.reshape(far, group, columns // 128, 128).transpose(0, 2, 1, 3).reshape(far, wt, 4, 128)
    dw_z = lax.all_to_all(dw_y, "zh", 0, 0, tiled=True)
    parts = [partial[0]] + [hop(partial[dx], -dx) for dx in range(1, blocks // 2)]
    other = []
    for part in parts:
        other.append(part[1:])
    across = swap(jnp.concatenate(other), "yl")
    (normed_grad,) = call(join_kernel, [((2, width, peers), bf16)], own, *parts, across)
    scale = float(rows * peers) ** (-0.5)
    grads = jnp.sum(dw_z.astype(f32), axis=0) * scale
    grads = grads.reshape(columns // 128, group, 128).transpose(1, 0, 2).reshape(group, columns)

    def restore(x):
        return x.transpose(2, 0, 1).reshape(1, peers, 2, width)

    return (restore(gated), grads[:, :width], grads[:, width:], restore(normed_grad))


def solution(mesh):
    mp = mesh.shape["mp"]
    far = mesh.shape["dp"] // 8
    fine = Mesh(mesh.devices.reshape(far, 2, 2, 2, mp // 2, 2), DP + MP)
    slots = P(DP, None, None, MP)
    weights = P(DP, MP)
    return jax.shard_map(
        body,
        mesh=fine,
        in_specs=(P(DP, MP), P(DP, None), P(DP), P(), weights, weights, slots),
        out_specs=(slots, weights, weights, slots),
        check_vma=False,
    )
```

```python
import jax
import jax.numpy as jnp
from jax import lax
from jax.experimental import pallas as pl
from jax.experimental.pallas import tpu as pltpu
from jax.sharding import Mesh, PartitionSpec as P


epsilon = 1e-05
bf16, f32, i32 = jnp.bfloat16, jnp.float32, jnp.int32
NEAR = ("zl", "yh")
DP = ("zh", "zl", "yh", "co")
MP = ("x", "yl")
INTERPRET = False


def nt(a, b):
    return lax.dot_general(a, b, (((1,), (1,)), ((), ())), preferred_element_type=f32)


def nn(a, b):
    return lax.dot_general(a, b, (((1,), (0,)), ((), ())), preferred_element_type=f32)


def tn(a, b):
    return lax.dot_general(a, b, (((0,), (0,)), ((), ())), preferred_element_type=f32)


def call(kernel, outs, *args, limit=12, scratch=(), away=False):
    vmem = pl.BlockSpec(memory_space=pltpu.VMEM)
    smem = pl.BlockSpec(memory_space=pltpu.SMEM)
    return pl.pallas_call(
        kernel,
        in_specs=[pl.BlockSpec(memory_space=pltpu.HBM) if away else smem if a.shape == (2,) else vmem for a in args],
        out_specs=[vmem] * len(outs),
        out_shape=[jax.ShapeDtypeStruct(s, d) for s, d in outs],
        scratch_shapes=list(scratch),
        compiler_params=pltpu.CompilerParams(vmem_limit_bytes=limit << 20),
        interpret=INTERPRET,
    )(*args)


def natural_of(p, co):
    core = (p // 96 + co) % 2
    return ((p // 12) % 2) * 96 + (((p // 24) % 4) * 2 + core) * 12 + p % 12


def send_kernel(frames_hbm, owner_hbm, valid_hbm, out_ref, frames_ref, owner_ref, valid_ref, sems):
    pairs = ((owner_hbm, owner_ref), (valid_hbm, valid_ref), (frames_hbm, frames_ref))
    copies = [pltpu.make_async_copy(a, b, sems.at[i]) for i, (a, b) in enumerate(pairs)]
    for copy in copies:
        copy.start()
    for copy in copies:
        copy.wait()
    rows, width = frames_ref.shape
    slots, lanes = out_ref.shape
    far = slots // 16
    owner = owner_ref[...]
    down = jnp.transpose(jnp.broadcast_to(owner, (rows, rows)))
    earlier = lax.broadcasted_iota(i32, (rows, rows), 0) < lax.broadcasted_iota(i32, (rows, rows), 1)
    slot = jnp.sum(jnp.where((down == owner) & earlier, 1.0, 0.0), axis=0, keepdims=True).astype(i32)
    place = ((owner % 8) * far + owner // 8) * 2 + slot
    hit = lax.broadcasted_iota(i32, (slots, rows), 0) == place
    placed = nn(jnp.where(hit, 1.0, 0.0).astype(bf16), frames_ref[...])
    live = jnp.sum(jnp.where(hit & (valid_ref[...] > 0), 1.0, 0.0), axis=1, keepdims=True)
    pad = lax.broadcasted_iota(i32, (slots, lanes - width), 1) == 0
    out_ref[...] = jnp.concatenate([placed, jnp.where(pad, live, 0.0)], axis=1).astype(bf16)


def turn_kernel(own_ref, rows_ref, out_ref, live_ref):
    width, slots = out_ref.shape
    peers = slots // 2
    lanes = rows_ref.shape[-1]
    place = lax.broadcasted_iota(i32, (width, lanes), 0)
    column = lax.broadcasted_iota(i32, (width, lanes), 1)
    pick = (column == natural_of(place, own_ref[1])).astype(bf16)
    flag = (lax.broadcasted_iota(i32, (16, lanes), 1) == width).astype(bf16)
    pick = jnp.concatenate([pick, flag], axis=0)
    source = lax.broadcasted_iota(i32, (slots, slots), 0)
    target = lax.broadcasted_iota(i32, (slots, slots), 1)
    order = (source == (target % peers) * 2 + target // peers).astype(bf16)
    ordered = nn(nt(pick, rows_ref[...]).astype(bf16), order)
    out_ref[...] = ordered[:width].astype(bf16)
    live_ref[...] = ordered[width : width + 8]


def block_of(own_ref, k, blocks):
    n = blocks // 2
    x, y = own_ref[0] // 2, own_ref[0] % 2
    return ((x + n - k % n) % n) * 2 + (y + k // n) % 2


def norm_kernel(own_ref, live_ref, gain_ref, *refs):
    near_refs, across_ref, normed_ref = refs[:-2], refs[-2], refs[-1]
    blocks, width, slots = normed_ref.shape
    total = blocks * width
    live = live_ref[0:1, :]

    def block(k):
        n = blocks // 2
        return (near_refs[k][...] if k < n else across_ref[k - n]).astype(f32)

    s = jnp.zeros((1, slots), f32)
    for k in range(blocks):
        s = s + jnp.sum(block(k), axis=0, keepdims=True)
    mean = s * (1.0 / total)
    s = jnp.zeros((1, slots), f32)
    for k in range(blocks):
        c = block(k) - mean
        s = s + jnp.sum(c * c, axis=0, keepdims=True)
    inv = lax.rsqrt(s * (1.0 / total) + epsilon)
    for k in range(blocks):
        c = block(k) - mean
        normed_ref[k] = (c * inv * gain_ref[block_of(own_ref, k, blocks)] * live).astype(bf16)


def w_block(wa_ref, wb_ref, m):
    return jnp.concatenate([ref[j, m] for ref in (wa_ref, wb_ref) for j in range(4)], axis=0)


def forward_kernel(own_ref, normed_ref, live_ref, wa_ref, wb_ref, up_ref, gated_ref, da_ref, db_ref, delta_ref):
    blocks, width, slots = normed_ref.shape
    peers = slots // 2
    live = live_ref[0:1, :]
    acc = jnp.zeros((2 * width, slots), f32)
    for k in range(blocks):
        acc = acc + tn(w_block(wa_ref, wb_ref, block_of(own_ref, k, blocks)), normed_ref[k])
    value, gate = acc[:width], acc[width:]
    sig = jax.nn.sigmoid(gate)
    up = jnp.concatenate([up_ref[0], up_ref[1]], axis=1).astype(f32)
    gated = (value * sig).astype(bf16)
    gated_ref[0] = gated[:, :peers]
    gated_ref[1] = gated[:, peers:]
    value_delta = (up * sig * live).astype(bf16)
    gate_delta = (up * value * sig * (1.0 - sig) * live).astype(bf16)
    delta = jnp.concatenate([value_delta, gate_delta], axis=0)
    delta_ref[...] = delta
    for k in range(blocks):
        dw = nt(normed_ref[k], delta)
        m = block_of(own_ref, k, blocks)
        for j in range(4):
            da_ref[j, m] = dw[24 * j : 24 * j + 24].astype(bf16)
            db_ref[j, m] = dw[24 * j + 96 : 24 * j + 120].astype(bf16)


def backward_kernel(own_ref, wa_ref, wb_ref, delta_ref, *partial_refs):
    blocks = 2 * len(partial_refs)
    for k in range(blocks):
        w = w_block(wa_ref, wb_ref, block_of(own_ref, k, blocks))
        partial_refs[k % (blocks // 2)][k // (blocks // 2)] = nn(w, delta_ref[...]).astype(bf16)


def join_kernel(own_ref, *refs):
    across_ref, out_ref = refs[-2:]
    width, slots = across_ref.shape[1:]
    peers = slots // 2
    s = jnp.zeros((width, slots), f32)
    for k, ref in enumerate(refs[:-2]):
        s = s + ref[0].astype(f32) + across_ref[k].astype(f32)
    place = lax.broadcasted_iota(i32, (width, width), 1)
    natural = lax.broadcasted_iota(i32, (width, width), 0)
    back = (natural_of(place, own_ref[1]) == natural).astype(bf16)
    out = nn(back, s.astype(bf16)).astype(bf16)
    out_ref[0] = out[:, :peers]
    out_ref[1] = out[:, peers:]


def spread(x, axis, count):
    return lax.all_to_all(jnp.broadcast_to(x[None], (count,) + x.shape), axis, 0, 0, tiled=True)


def hop(x, step):
    n = lax.axis_size("x")
    return lax.ppermute(x, "x", [(i, (i + step) % n) for i in range(n)])


def swap(x, axis):
    return lax.ppermute(x, axis, [(0, 1), (1, 0)])


def stay(x):
    return x if INTERPRET else pltpu.with_memory_space_constraint(x, pltpu.HBM)


def tiles(x):
    return x.reshape(x.shape[0] // 4, 4, x.shape[1] // 128, 128).transpose(2, 0, 1, 3)


def body(frames, frame_owner, frame_valid, norm_gain, value_weight, gate_weight, grad_owned):
    far = lax.axis_size("zh")
    blocks = lax.axis_size(MP)
    peers = 8 * far
    slots = 2 * peers
    rows, width = frames.shape
    group = value_weight.shape[0]
    columns = 2 * width
    wt = columns // 128 * group // 4
    lanes = -(-(width + 1) // 128) * 128
    halves = lanes // 128
    core = lax.axis_index("co").astype(i32)
    own = jnp.stack([lax.axis_index(MP).astype(i32), core])

    (sent,) = call(
        send_kernel,
        [((slots, lanes), bf16)],
        *map(stay, (frames, frame_owner.reshape(1, rows), frame_valid.reshape(1, rows))),
        scratch=[
            pltpu.VMEM((rows, width), bf16),
            pltpu.VMEM((1, rows), i32),
            pltpu.VMEM((1, rows), i32),
            pltpu.SemaphoreType.DMA((3,)),
        ],
        away=True,
    )
    sent = lax.all_to_all(sent.reshape(8, 2 * far, lanes), ("zl", "yh", "co"), 0, 0, tiled=True)
    shard = tiles(jnp.concatenate([value_weight, gate_weight], axis=1)).reshape(wt, 4, 128)
    shard = jnp.broadcast_to(shard[None], (far,) + shard.shape)
    sent = sent.reshape(8, far, 2, halves, 128).transpose(1, 3, 0, 2, 4).reshape(far, 4 * halves, 4, 128)
    got = lax.all_to_all(jnp.concatenate([shard, sent], axis=1), "zh", 0, 0, tiled=True)
    rows_z = got[:, wt:].reshape(far, halves, 16, 128).transpose(0, 2, 1, 3).reshape(slots, lanes)
    w_rows = got[:, :wt].reshape(far, columns // 128, group, 128).transpose(0, 2, 1, 3)
    w_rows = w_rows.reshape(far * group, columns)
    w_own = spread(w_rows, NEAR, 4)
    w_other = swap(w_own, "co")
    w_own = w_own.reshape(4, blocks, 2 * group, columns)
    w_other = w_other.reshape(4, blocks, 2 * group, columns)
    turned, live = call(
        turn_kernel,
        [((width, slots), bf16), ((8, slots), f32)],
        own,
        rows_z,
    )
    whole = [turned] + [hop(turned, dx) for dx in range(1, blocks // 2)]
    stacked = jnp.stack(whole)
    whole.append(swap(stacked, "yl"))
    gain = norm_gain.reshape(blocks, 2, 4, 2, 12).transpose(0, 3, 2, 1, 4)
    gain = jnp.where(core == 0, gain, gain[:, ::-1]).reshape(blocks, width, 1)
    (normed,) = call(norm_kernel, [((blocks, width, slots), bf16)], own, live, gain, *whole)
    up = grad_owned.reshape(peers, 2, width).transpose(1, 2, 0)
    near = (4, blocks, 2 * group, columns)
    gated, dw_own, dw_other, delta = call(
        forward_kernel,
        [((2, width, peers), bf16), (near, bf16), (near, bf16), ((columns, slots), bf16)],
        own,
        normed,
        live,
        w_own,
        w_other,
        up,
    )
    dw_c = swap(dw_other.reshape(4, far * group, columns), "co")
    partial = call(
        backward_kernel, [((2, width, slots), bf16)] * (blocks // 2), own, w_own, w_other, delta
    )
    dw_c = (dw_c.astype(f32) + dw_own.reshape(4, far * group, columns).astype(f32)).astype(bf16)
    dw_y = lax.all_to_all(dw_c, NEAR, 0, 0, tiled=True)
    dw_y = jnp.sum(dw_y.astype(f32), axis=0).astype(bf16)
    dw_y = dw_y.reshape(far, group, columns // 128, 128).transpose(0, 2, 1, 3).reshape(far, wt, 4, 128)
    dw_z = lax.all_to_all(dw_y, "zh", 0, 0, tiled=True)
    parts = [partial[0]] + [hop(partial[dx], -dx) for dx in range(1, blocks // 2)]
    other = []
    for part in parts:
        other.append(part[1:])
    across = swap(jnp.concatenate(other), "yl")
    (normed_grad,) = call(join_kernel, [((2, width, peers), bf16)], own, *parts, across)
    scale = float(rows * peers) ** (-0.5)
    grads = jnp.sum(dw_z.astype(f32), axis=0) * scale
    grads = grads.reshape(columns // 128, group, 128).transpose(1, 0, 2).reshape(group, columns)

    def restore(x):
        return x.transpose(2, 0, 1).reshape(1, peers, 2, width)

    return (restore(gated), grads[:, :width], grads[:, width:], restore(normed_grad))


def solution(mesh):
    mp = mesh.shape["mp"]
    far = mesh.shape["dp"] // 8
    fine = Mesh(mesh.devices.reshape(far, 2, 2, 2, mp // 2, 2), DP + MP)
    slots = P(DP, None, None, MP)
    weights = P(DP, MP)
    return jax.shard_map(
        body,
        mesh=fine,
        in_specs=(P(DP, MP), P(DP, None), P(DP), P(), weights, weights, slots),
        out_specs=(slots, weights, weights, slots),
        check_vma=False,
    )
```

```python
import jax
import jax.numpy as jnp
from jax import lax
from jax.experimental import pallas as pl
from jax.experimental.pallas import tpu as pltpu
from jax.sharding import Mesh, PartitionSpec as P


epsilon = 1e-05
bf16, f32, i32 = jnp.bfloat16, jnp.float32, jnp.int32
NEAR = ("zl", "yh")
DP = ("zh", "zl", "yh", "co")
MP = ("x", "yl")
INTERPRET = False


def nt(a, b):
    return lax.dot_general(a, b, (((1,), (1,)), ((), ())), preferred_element_type=f32)


def nn(a, b):
    return lax.dot_general(a, b, (((1,), (0,)), ((), ())), preferred_element_type=f32)


def tn(a, b):
    return lax.dot_general(a, b, (((0,), (0,)), ((), ())), preferred_element_type=f32)


def call(kernel, outs, *args, limit=12, scratch=(), away=False):
    vmem = pl.BlockSpec(memory_space=pltpu.VMEM)
    smem = pl.BlockSpec(memory_space=pltpu.SMEM)
    return pl.pallas_call(
        kernel,
        in_specs=[pl.BlockSpec(memory_space=pltpu.HBM) if away else smem if a.shape == (2,) else vmem for a in args],
        out_specs=[vmem] * len(outs),
        out_shape=[jax.ShapeDtypeStruct(s, d) for s, d in outs],
        scratch_shapes=list(scratch),
        compiler_params=pltpu.CompilerParams(vmem_limit_bytes=limit << 20),
        interpret=INTERPRET,
    )(*args)


def natural_of(p, co):
    core = (p // 96 + co) % 2
    return ((p // 12) % 2) * 96 + (((p // 24) % 4) * 2 + core) * 12 + p % 12


def send_kernel(frames_hbm, owner_hbm, valid_hbm, out_ref, frames_ref, owner_ref, valid_ref, sems):
    pairs = ((owner_hbm, owner_ref), (valid_hbm, valid_ref), (frames_hbm, frames_ref))
    copies = [pltpu.make_async_copy(a, b, sems.at[i]) for i, (a, b) in enumerate(pairs)]
    for copy in copies:
        copy.start()
    for copy in copies:
        copy.wait()
    rows, width = frames_ref.shape
    slots, lanes = out_ref.shape
    owner = owner_ref[...]
    down = jnp.transpose(jnp.broadcast_to(owner, (rows, rows)))
    earlier = lax.broadcasted_iota(i32, (rows, rows), 0) < lax.broadcasted_iota(i32, (rows, rows), 1)
    slot = jnp.sum(jnp.where((down == owner) & earlier, 1.0, 0.0), axis=0, keepdims=True).astype(i32)
    hit = lax.broadcasted_iota(i32, (slots, rows), 0) == owner * 2 + slot
    placed = nn(jnp.where(hit, 1.0, 0.0).astype(bf16), frames_ref[...])
    live = jnp.sum(jnp.where(hit & (valid_ref[...] > 0), 1.0, 0.0), axis=1, keepdims=True)
    pad = lax.broadcasted_iota(i32, (slots, lanes - width), 1) == 0
    out_ref[...] = jnp.concatenate([placed, jnp.where(pad, live, 0.0)], axis=1).astype(bf16)


def turn_kernel(own_ref, rows_ref, out_ref, live_ref):
    width, slots = out_ref.shape[1:]
    peers = slots // 2
    far = peers // 8
    lanes = rows_ref.shape[-1]
    place = lax.broadcasted_iota(i32, (width, lanes), 0)
    column = lax.broadcasted_iota(i32, (width, lanes), 1)
    pick = (column == natural_of(place, own_ref[1])).astype(bf16)
    flag = (lax.broadcasted_iota(i32, (16, lanes), 1) == width).astype(bf16)
    pick = jnp.concatenate([pick, flag], axis=0)
    source = lax.broadcasted_iota(i32, (slots, slots), 0)
    target = lax.broadcasted_iota(i32, (slots, slots), 1)
    loader = target % peers
    order = (source == ((loader % 8) * far + loader // 8) * 2 + target // peers).astype(bf16)
    for y in range(2):
        rows = jnp.concatenate([rows_ref[n, y] for n in range(8)], axis=0)
        ordered = nn(nt(pick, rows).astype(bf16), order)
        out_ref[y] = ordered[:width].astype(bf16)
    live_ref[...] = ordered[width : width + 8]


def block_of(own_ref, k, blocks, relative=False):
    x, y = own_ref[0] // 2, own_ref[0] % 2
    y = (y + k) % 2 if relative else k % 2
    return ((x + (blocks // 2 - k // 2)) % (blocks // 2)) * 2 + y


def norm_kernel(own_ref, live_ref, gain_ref, *refs):
    normed_ref = refs[-1]
    blocks, width, slots = normed_ref.shape
    total = blocks * width
    live = live_ref[0:1, :]
    s = jnp.zeros((1, slots), f32)
    for k in range(blocks):
        s = s + jnp.sum(refs[k // 2][k % 2].astype(f32), axis=0, keepdims=True)
    mean = s * (1.0 / total)
    s = jnp.zeros((1, slots), f32)
    for k in range(blocks):
        c = refs[k // 2][k % 2].astype(f32) - mean
        s = s + jnp.sum(c * c, axis=0, keepdims=True)
    inv = lax.rsqrt(s * (1.0 / total) + epsilon)
    for k in range(blocks):
        c = refs[k // 2][k % 2].astype(f32) - mean
        normed_ref[k] = (c * inv * gain_ref[block_of(own_ref, k, blocks)] * live).astype(bf16)


def w_block(wa_ref, wb_ref, m):
    return jnp.concatenate([ref[j, m] for ref in (wa_ref, wb_ref) for j in range(4)], axis=0)


def forward_kernel(own_ref, normed_ref, live_ref, wa_ref, wb_ref, up_ref, gated_ref, da_ref, db_ref, delta_ref):
    blocks, width, slots = normed_ref.shape
    peers = slots // 2
    live = live_ref[0:1, :]
    acc = jnp.zeros((2 * width, slots), f32)
    for k in range(blocks):
        acc = acc + tn(w_block(wa_ref, wb_ref, block_of(own_ref, k, blocks)), normed_ref[k])
    value, gate = acc[:width], acc[width:]
    sig = jax.nn.sigmoid(gate)
    up = jnp.concatenate([up_ref[0], up_ref[1]], axis=1).astype(f32)
    gated = (value * sig).astype(bf16)
    gated_ref[0] = gated[:, :peers]
    gated_ref[1] = gated[:, peers:]
    value_delta = (up * sig * live).astype(bf16)
    gate_delta = (up * value * sig * (1.0 - sig) * live).astype(bf16)
    delta = jnp.concatenate([value_delta, gate_delta], axis=0)
    delta_ref[...] = delta
    for k in range(blocks):
        dw = nt(normed_ref[k], delta)
        m = block_of(own_ref, k, blocks)
        for j in range(4):
            da_ref[j, m] = dw[24 * j : 24 * j + 24].astype(bf16)
            db_ref[j, m] = dw[24 * j + 96 : 24 * j + 120].astype(bf16)


def backward_kernel(own_ref, wa_ref, wb_ref, delta_ref, *partial_refs):
    blocks = 2 * len(partial_refs)
    for k in range(blocks):
        w = w_block(wa_ref, wb_ref, block_of(own_ref, k, blocks, True))
        partial_refs[k // 2][k % 2] = nn(w, delta_ref[...]).astype(bf16)


def join_kernel(own_ref, *refs):
    across_ref, out_ref = refs[-2:]
    width, slots = across_ref.shape[1:]
    peers = slots // 2
    s = jnp.zeros((width, slots), f32)
    for k, ref in enumerate(refs[:-2]):
        s = s + ref[0].astype(f32) + across_ref[k].astype(f32)
    place = lax.broadcasted_iota(i32, (width, width), 1)
    natural = lax.broadcasted_iota(i32, (width, width), 0)
    back = (natural_of(place, own_ref[1]) == natural).astype(bf16)
    out = nn(back, s.astype(bf16)).astype(bf16)
    out_ref[0] = out[:, :peers]
    out_ref[1] = out[:, peers:]


def spread(x, axis, count):
    return lax.all_to_all(jnp.broadcast_to(x[None], (count,) + x.shape), axis, 0, 0, tiled=True)


def hop(x, step):
    n = lax.axis_size("x")
    return lax.ppermute(x, "x", [(i, (i + step) % n) for i in range(n)])


def swap(x, axis):
    return lax.ppermute(x, axis, [(0, 1), (1, 0)])


def stay(x):
    return x if INTERPRET else pltpu.with_memory_space_constraint(x, pltpu.HBM)


def tiles(x):
    return x.reshape(x.shape[0] // 4, 4, x.shape[1] // 128, 128).transpose(2, 0, 1, 3)


def body(frames, frame_owner, frame_valid, norm_gain, value_weight, gate_weight, grad_owned):
    far = lax.axis_size("zh")
    blocks = lax.axis_size(MP)
    peers = 8 * far
    slots = 2 * peers
    rows, width = frames.shape
    group = value_weight.shape[0]
    columns = 2 * width
    wt = columns // 128 * group // 4
    lanes = -(-(width + 1) // 128) * 128
    halves = lanes // 128
    core = lax.axis_index("co").astype(i32)
    own = jnp.stack([lax.axis_index(MP).astype(i32), core])

    shard = tiles(jnp.concatenate([value_weight, gate_weight], axis=1)).reshape(wt, 4, 128)
    (sent,) = call(
        send_kernel,
        [((slots, lanes), bf16)],
        *map(stay, (frames, frame_owner.reshape(1, rows), frame_valid.reshape(1, rows))),
        scratch=[
            pltpu.VMEM((rows, width), bf16),
            pltpu.VMEM((1, rows), i32),
            pltpu.VMEM((1, rows), i32),
            pltpu.SemaphoreType.DMA((3,)),
        ],
        away=True,
    )
    sent = sent.reshape(far, 4, 4, halves, 128).transpose(0, 3, 1, 2, 4).reshape(far, 4 * halves, 4, 128)
    sent = jnp.concatenate([jnp.broadcast_to(shard[None], (far,) + shard.shape), sent], axis=1)
    got = lax.all_to_all(sent, "zh", 0, 0, tiled=True)
    rows_z = got[:, wt:].reshape(far, halves, 8, 2, 128).transpose(2, 0, 3, 1, 4).reshape(8, 1, 2 * far, lanes)
    rows_z = jnp.broadcast_to(rows_z, (8, 2, 2 * far, lanes)).reshape(16, 2 * far, lanes)
    rows_y = lax.all_to_all(rows_z, ("zl", "yh", "co", "yl"), 0, 0, tiled=True)
    w_rows = got[:, :wt].reshape(far, columns // 128, group, 128).transpose(0, 2, 1, 3)
    w_rows = w_rows.reshape(far * group, columns)
    w_own = spread(w_rows, NEAR, 4)
    w_other = swap(w_own, "co")
    w_own = w_own.reshape(4, blocks, 2 * group, columns)
    w_other = w_other.reshape(4, blocks, 2 * group, columns)
    turned, live = call(
        turn_kernel,
        [((2, width, slots), bf16), ((8, slots), f32)],
        own,
        rows_y.reshape(8, 2, 2 * far, lanes),
    )
    whole = [turned] + [hop(turned, dx) for dx in range(1, blocks // 2)]
    gain = norm_gain.reshape(blocks, 2, 4, 2, 12).transpose(0, 3, 2, 1, 4)
    gain = jnp.where(core == 0, gain, gain[:, ::-1]).reshape(blocks, width, 1)
    (normed,) = call(norm_kernel, [((blocks, width, slots), bf16)], own, live, gain, *whole)
    up = grad_owned.reshape(peers, 2, width).transpose(1, 2, 0)
    near = (4, blocks, 2 * group, columns)
    gated, dw_own, dw_other, delta = call(
        forward_kernel,
        [((2, width, peers), bf16), (near, bf16), (near, bf16), ((columns, slots), bf16)],
        own,
        normed,
        live,
        w_own,
        w_other,
        up,
    )
    dw_c = swap(dw_other.reshape(4, far * group, columns), "co")
    partial = call(
        backward_kernel, [((2, width, slots), bf16)] * (blocks // 2), own, w_own, w_other, delta
    )
    dw_c = (dw_c.astype(f32) + dw_own.reshape(4, far * group, columns).astype(f32)).astype(bf16)
    dw_y = lax.all_to_all(dw_c, NEAR, 0, 0, tiled=True)
    dw_y = jnp.sum(dw_y.astype(f32), axis=0).astype(bf16)
    dw_y = dw_y.reshape(far, group, columns // 128, 128).transpose(0, 2, 1, 3).reshape(far, wt, 4, 128)
    dw_z = lax.all_to_all(dw_y, "zh", 0, 0, tiled=True)
    parts = [partial[0]] + [hop(partial[dx], -dx) for dx in range(1, blocks // 2)]
    other = []
    for part in parts:
        other.append(part[1:])
    across = swap(jnp.concatenate(other), "yl")
    (normed_grad,) = call(join_kernel, [((2, width, peers), bf16)], own, *parts, across)
    scale = float(rows * peers) ** (-0.5)
    grads = jnp.sum(dw_z.astype(f32), axis=0) * scale
    grads = grads.reshape(columns // 128, group, 128).transpose(1, 0, 2).reshape(group, columns)

    def restore(x):
        return x.transpose(2, 0, 1).reshape(1, peers, 2, width)

    return (restore(gated), grads[:, :width], grads[:, width:], restore(normed_grad))


def solution(mesh):
    mp = mesh.shape["mp"]
    far = mesh.shape["dp"] // 8
    fine = Mesh(mesh.devices.reshape(far, 2, 2, 2, mp // 2, 2), DP + MP)
    slots = P(DP, None, None, MP)
    weights = P(DP, MP)
    return jax.shard_map(
        body,
        mesh=fine,
        in_specs=(P(DP, MP), P(DP, None), P(DP), P(), weights, weights, slots),
        out_specs=(slots, weights, weights, slots),
        check_vma=False,
    )
```

```python
import jax
import jax.numpy as jnp
from jax import lax
from jax.experimental import pallas as pl
from jax.experimental.pallas import tpu as pltpu
from jax.sharding import Mesh, PartitionSpec as P


epsilon = 1e-05
bf16, f32, i32 = jnp.bfloat16, jnp.float32, jnp.int32
NEAR = ("zl", "yh")
DP = ("zh", "zl", "yh", "co")
MP = ("x", "yl")
INTERPRET = False


def nt(a, b):
    return lax.dot_general(a, b, (((1,), (1,)), ((), ())), preferred_element_type=f32)


def nn(a, b):
    return lax.dot_general(a, b, (((1,), (0,)), ((), ())), preferred_element_type=f32)


def tn(a, b):
    return lax.dot_general(a, b, (((0,), (0,)), ((), ())), preferred_element_type=f32)


def call(kernel, outs, *args, limit=12, scratch=(), away=False):
    vmem = pl.BlockSpec(memory_space=pltpu.VMEM)
    smem = pl.BlockSpec(memory_space=pltpu.SMEM)
    return pl.pallas_call(
        kernel,
        in_specs=[pl.BlockSpec(memory_space=pltpu.HBM) if away else smem if a.shape == (2,) else vmem for a in args],
        out_specs=[vmem] * len(outs),
        out_shape=[jax.ShapeDtypeStruct(s, d) for s, d in outs],
        scratch_shapes=list(scratch),
        compiler_params=pltpu.CompilerParams(vmem_limit_bytes=limit << 20),
        interpret=INTERPRET,
    )(*args)


def row_order(p):
    return (p % 16) * 12 + (p // 48) * 3 + (p // 16) % 3


def owner_order(p, co):
    core = (p // 96 + co) % 2
    return ((p // 12) % 2) * 96 + (((p // 24) % 4) * 2 + core) * 12 + p % 12


def send_kernel(frames_hbm, owner_hbm, valid_hbm, vw_hbm, gw_hbm, out_ref, frames_ref, owner_ref, valid_ref, vw_ref, gw_ref, sems):
    pairs = ((owner_hbm, owner_ref), (valid_hbm, valid_ref), (frames_hbm, frames_ref), (vw_hbm, vw_ref), (gw_hbm, gw_ref))
    copies = [pltpu.make_async_copy(a, b, sems.at[i]) for i, (a, b) in enumerate(pairs)]
    for copy in copies:
        copy.start()
    for copy in copies:
        copy.wait()
    rows, _ = frames_ref.shape
    peers = out_ref.shape[1]
    owner = owner_ref[...]
    down = jnp.transpose(jnp.broadcast_to(owner, (rows, rows)))
    earlier = lax.broadcasted_iota(i32, (rows, rows), 0) < lax.broadcasted_iota(i32, (rows, rows), 1)
    slot = jnp.sum(jnp.where((down == owner) & earlier, 1.0, 0.0), axis=0, keepdims=True).astype(i32)
    hit = lax.broadcasted_iota(i32, (2 * peers, rows), 0) == slot * peers + owner
    placed = nn(jnp.where(hit, 1.0, 0.0).astype(bf16), frames_ref[...])
    live = jnp.sum(jnp.where(hit & (valid_ref[...] > 0), 1.0, 0.0), axis=1, keepdims=True)
    first, second = placed[:peers], placed[peers:]
    out_ref[0] = first[:, :128].astype(bf16)
    out_ref[1] = second[:, :128].astype(bf16)
    out_ref[2] = jnp.concatenate([first[:, 128:], second[:, 128:]], axis=1).astype(bf16)
    shard = jnp.concatenate([vw_ref[...].astype(f32), gw_ref[...].astype(f32)], axis=1)

    def lines(units):
        picked = [shard[3 * q + u // 3 : 3 * q + u // 3 + 1, 128 * (u % 3) : 128 * (u % 3) + 128] for q, u in units]
        return jnp.concatenate([jnp.concatenate(picked, axis=0)] * (peers // 8), axis=0)

    for k in range(4):
        out_ref[3 + k] = lines([(n // 2, 4 * (n % 2) + k) for n in range(8)]).astype(bf16)
    last = lines([(n // 2, 8) for n in range(8)])
    core = lax.broadcasted_iota(i32, (peers, 128), 0) % 2
    lane = lax.broadcasted_iota(i32, (peers, 128), 1)
    flag = lane - 64 * (1 - core)
    flags = jnp.where(flag == 0, live[:peers], 0.0) + jnp.where(flag == 1, live[peers:], 0.0)
    out_ref[7] = jnp.where(lane // 64 == core, last, flags).astype(bf16)


def turn_kernel(own_ref, rows_ref, out_ref, live_ref):
    width, slots = out_ref.shape
    peers = slots // 2
    channel = row_order(lax.broadcasted_iota(i32, (width, 128), 0))
    lane = lax.broadcasted_iota(i32, (width, 128), 1)
    low = (lane == channel).astype(bf16)
    at = lax.broadcasted_iota(i32, (16, 128), 1)
    for c in range(2):
        high = (lane == channel - 128 + 64 * c).astype(bf16)
        high = jnp.where((channel >= 128), high.astype(f32), 0.0).astype(bf16)
        turned = nt(low, rows_ref[c]) + nt(high, rows_ref[2])
        out_ref[:, c * peers : (c + 1) * peers] = turned.astype(bf16)
        flag = (at == 64 * (1 - own_ref[1]) + c).astype(bf16)
        live_ref[:, c * peers : (c + 1) * peers] = nt(flag, rows_ref[7])[:8]


def block_of(own_ref, k, blocks):
    n = blocks // 2
    x, y = own_ref[0] // 2, own_ref[0] % 2
    return ((x + n - k % n) % n) * 2 + (y + k // n) % 2


def norm_kernel(own_ref, live_ref, gain_ref, *refs):
    near_refs, across_ref, normed_ref = refs[:-2], refs[-2], refs[-1]
    blocks, width, slots = normed_ref.shape
    total = blocks * width
    live = live_ref[0:1, :]

    def block(k):
        n = blocks // 2
        return (near_refs[k][...] if k < n else across_ref[k - n]).astype(f32)

    s = jnp.zeros((1, slots), f32)
    for k in range(blocks):
        s = s + jnp.sum(block(k), axis=0, keepdims=True)
    mean = s * (1.0 / total)
    s = jnp.zeros((1, slots), f32)
    for k in range(blocks):
        c = block(k) - mean
        s = s + jnp.sum(c * c, axis=0, keepdims=True)
    inv = lax.rsqrt(s * (1.0 / total) + epsilon)
    for k in range(blocks):
        c = block(k) - mean
        normed_ref[k] = (c * inv * gain_ref[block_of(own_ref, k, blocks)] * live).astype(bf16)


def forward_kernel(own_ref, normed_ref, live_ref, wa_ref, wb_ref, up_ref, gated_ref, da_ref, db_ref, delta_ref, w_ref):
    blocks, width, slots = normed_ref.shape
    peers = slots // 2
    live = live_ref[0:1, :]
    first = own_ref[1] == 0
    lane = lax.broadcasted_iota(i32, (16, 128), 1)

    def unit(q, u, m):
        at = pl.ds(pl.multiple_of(16 * m, 16), 16)
        a, b = wa_ref[q, u % 4 if u < 8 else 4, at, :], wb_ref[q, u % 4 if u < 8 else 4, at, :]
        if u < 4:
            return jnp.where(first, a, b)
        if u < 8:
            return jnp.where(first, b, a)
        low, high = jnp.where(first, a, b).astype(f32), jnp.where(first, b, a).astype(f32)
        return jnp.where(lane < 64, low, high).astype(bf16)

    acc = jnp.zeros((2 * width, slots), f32)
    for k in range(blocks):
        m = block_of(own_ref, k, blocks)
        for q in range(4):
            for r in range(3):
                row = 48 * q + 16 * r
                w_ref[k, row : row + 16, :] = jnp.concatenate([unit(q, 3 * r + i, m) for i in range(3)], axis=1)
        acc = acc + tn(w_ref[k], normed_ref[k])
    value, gate = acc[:width], acc[width:]
    sig = jax.nn.sigmoid(gate)
    up = jnp.concatenate([up_ref[0], up_ref[1]], axis=1).astype(f32)
    gated = (value * sig).astype(bf16)
    gated_ref[0] = gated[:, :peers]
    gated_ref[1] = gated[:, peers:]
    value_delta = (up * sig * live).astype(bf16)
    gate_delta = (up * value * sig * (1.0 - sig) * live).astype(bf16)
    delta = jnp.concatenate([value_delta, gate_delta], axis=0)
    delta_ref[...] = delta
    target = owner_order(lax.broadcasted_iota(i32, (width, width), 0), own_ref[1])
    move = (target == row_order(lax.broadcasted_iota(i32, (width, width), 1))).astype(bf16)
    for k in range(blocks):
        dw = nt(nn(move, normed_ref[k]).astype(bf16), delta)
        m = block_of(own_ref, k, blocks)
        for j in range(4):
            da_ref[j, m] = dw[24 * j : 24 * j + 24].astype(bf16)
            db_ref[j, m] = dw[24 * j + 96 : 24 * j + 120].astype(bf16)


def backward_kernel(w_ref, delta_ref, *partial_refs):
    blocks = 2 * len(partial_refs)
    for k in range(blocks):
        n = blocks // 2
        partial_refs[k % n][k // n] = nn(w_ref[k], delta_ref[...]).astype(bf16)


def join_kernel(*refs):
    across_ref, out_ref = refs[-2:]
    width, slots = across_ref.shape[1:]
    peers = slots // 2
    s = jnp.zeros((width, slots), f32)
    for k, ref in enumerate(refs[:-2]):
        s = s + ref[0].astype(f32) + across_ref[k].astype(f32)
    place = lax.broadcasted_iota(i32, (width, width), 1)
    natural = lax.broadcasted_iota(i32, (width, width), 0)
    back = (row_order(place) == natural).astype(bf16)
    out = nn(back, s.astype(bf16)).astype(bf16)
    out_ref[0] = out[:, :peers]
    out_ref[1] = out[:, peers:]


def spread(x, axis, count):
    return lax.all_to_all(jnp.broadcast_to(x[None], (count,) + x.shape), axis, 0, 0, tiled=True)


def hop(x, step):
    n = lax.axis_size("x")
    return lax.ppermute(x, "x", [(i, (i + step) % n) for i in range(n)])


def swap(x, axis):
    return lax.ppermute(x, axis, [(0, 1), (1, 0)])


def stay(x):
    return x if INTERPRET else pltpu.with_memory_space_constraint(x, pltpu.HBM)


def body(frames, frame_owner, frame_valid, norm_gain, value_weight, gate_weight, grad_owned):
    far = lax.axis_size("zh")
    blocks = lax.axis_size(MP)
    peers = 8 * far
    slots = 2 * peers
    rows, width = frames.shape
    group = value_weight.shape[0]
    columns = 2 * width
    wt = columns // 128 * group // 4
    core = lax.axis_index("co").astype(i32)
    own = jnp.stack([lax.axis_index(MP).astype(i32), core])

    (sent,) = call(
        send_kernel,
        [((8, peers, 128), bf16)],
        *map(stay, (frames, frame_owner.reshape(1, rows), frame_valid.reshape(1, rows), value_weight, gate_weight)),
        scratch=[
            pltpu.VMEM((rows, width), bf16),
            pltpu.VMEM((1, rows), i32),
            pltpu.VMEM((1, rows), i32),
            pltpu.VMEM((group, width), bf16),
            pltpu.VMEM((group, width), bf16),
            pltpu.SemaphoreType.DMA((5,)),
        ],
        away=True,
    )
    got = lax.all_to_all(sent.transpose(1, 0, 2), DP, 0, 0, tiled=True)
    got = got.transpose(1, 0, 2)
    w_own = spread(got[3:], NEAR, 4)
    w_other = swap(w_own, "co")
    turned, live = call(turn_kernel, [((width, slots), bf16), ((8, slots), f32)], own, got)
    whole = [turned] + [hop(turned, dx) for dx in range(1, blocks // 2)]
    stacked = jnp.stack(whole)
    whole.append(swap(stacked, "yl"))
    gain = norm_gain.reshape(blocks, 16, 4, 3).transpose(0, 2, 3, 1).reshape(blocks, width, 1)
    (normed,) = call(norm_kernel, [((blocks, width, slots), bf16)], own, live, gain, *whole)
    up = grad_owned.reshape(peers, 2, width).transpose(1, 2, 0)
    near = (4, blocks, 2 * group, columns)
    gated, dw_own, dw_other, delta, w_all = call(
        forward_kernel,
        [((2, width, peers), bf16), (near, bf16), (near, bf16), ((columns, slots), bf16), ((blocks, width, columns), bf16)],
        own,
        normed,
        live,
        w_own,
        w_other,
        up,
    )
    dw_c = swap(dw_other.reshape(4, far * group, columns), "co")
    partial = call(backward_kernel, [((2, width, slots), bf16)] * (blocks // 2), w_all, delta)
    dw_c = (dw_c.astype(f32) + dw_own.reshape(4, far * group, columns).astype(f32)).astype(bf16)
    dw_y = lax.all_to_all(dw_c, NEAR, 0, 0, tiled=True)
    dw_y = jnp.sum(dw_y.astype(f32), axis=0).astype(bf16)
    dw_y = dw_y.reshape(far, group, columns // 128, 128).transpose(0, 2, 1, 3).reshape(far, wt, 4, 128)
    dw_z = lax.all_to_all(dw_y, "zh", 0, 0, tiled=True)
    parts = [partial[0]] + [hop(partial[dx], -dx) for dx in range(1, blocks // 2)]
    other = []
    for part in parts:
        other.append(part[1:])
    across = swap(jnp.concatenate(other), "yl")
    (normed_grad,) = call(join_kernel, [((2, width, peers), bf16)], *parts, across)
    scale = float(rows * peers) ** (-0.5)
    grads = jnp.sum(dw_z.astype(f32), axis=0) * scale
    grads = grads.reshape(columns // 128, group, 128).transpose(1, 0, 2).reshape(group, columns)

    def restore(x):
        return x.transpose(2, 0, 1).reshape(1, peers, 2, width)

    return (restore(gated), grads[:, :width], grads[:, width:], restore(normed_grad))


def solution(mesh):
    mp = mesh.shape["mp"]
    far = mesh.shape["dp"] // 8
    fine = Mesh(mesh.devices.reshape(far, 2, 2, 2, mp // 2, 2), DP + MP)
    slots = P(DP, None, None, MP)
    weights = P(DP, MP)
    return jax.shard_map(
        body,
        mesh=fine,
        in_specs=(P(DP, MP), P(DP, None), P(DP), P(), weights, weights, slots),
        out_specs=(slots, weights, weights, slots),
        check_vma=False,
    )
```

```python
import jax
import jax.numpy as jnp
from jax import lax
from jax.experimental import pallas as pl
from jax.experimental.pallas import tpu as pltpu
from jax.sharding import Mesh, PartitionSpec as P


epsilon = 1e-05
bf16, f32, i32 = jnp.bfloat16, jnp.float32, jnp.int32
NEAR = ("zl", "yh")
DP = ("zh", "zl", "yh", "co")
MP = ("x", "yl")
INTERPRET = False


def nt(a, b):
    return lax.dot_general(a, b, (((1,), (1,)), ((), ())), preferred_element_type=f32)


def nn(a, b):
    return lax.dot_general(a, b, (((1,), (0,)), ((), ())), preferred_element_type=f32)


def tn(a, b):
    return lax.dot_general(a, b, (((0,), (0,)), ((), ())), preferred_element_type=f32)


def call(kernel, outs, *args, limit=12, scratch=(), away=False):
    vmem = pl.BlockSpec(memory_space=pltpu.VMEM)
    smem = pl.BlockSpec(memory_space=pltpu.SMEM)
    return pl.pallas_call(
        kernel,
        in_specs=[pl.BlockSpec(memory_space=pltpu.HBM) if away else smem if a.shape == (2,) else vmem for a in args],
        out_specs=[vmem] * len(outs),
        out_shape=[jax.ShapeDtypeStruct(s, d) for s, d in outs],
        scratch_shapes=list(scratch),
        compiler_params=pltpu.CompilerParams(vmem_limit_bytes=limit << 20),
        interpret=INTERPRET,
    )(*args)


def row_order(p):
    return (p % 16) * 12 + (p // 48) * 3 + (p // 16) % 3


def owner_order(p, co):
    core = (p // 96 + co) % 2
    return ((p // 12) % 2) * 96 + (((p // 24) % 4) * 2 + core) * 12 + p % 12


def send_kernel(frames_hbm, owner_hbm, valid_hbm, vw_hbm, gw_hbm, out_ref, frames_ref, owner_ref, valid_ref, vw_ref, gw_ref, sems):
    pairs = ((owner_hbm, owner_ref), (valid_hbm, valid_ref), (frames_hbm, frames_ref), (vw_hbm, vw_ref), (gw_hbm, gw_ref))
    copies = [pltpu.make_async_copy(a, b, sems.at[i]) for i, (a, b) in enumerate(pairs)]
    for copy in copies:
        copy.start()
    for copy in copies:
        copy.wait()
    rows, _ = frames_ref.shape
    peers = out_ref.shape[1]
    owner = owner_ref[...]
    down = jnp.transpose(jnp.broadcast_to(owner, (rows, rows)))
    earlier = lax.broadcasted_iota(i32, (rows, rows), 0) < lax.broadcasted_iota(i32, (rows, rows), 1)
    slot = jnp.sum(jnp.where((down == owner) & earlier, 1.0, 0.0), axis=0, keepdims=True).astype(i32)
    hit = lax.broadcasted_iota(i32, (2 * peers, rows), 0) == slot * peers + owner
    placed = nn(jnp.where(hit, 1.0, 0.0).astype(bf16), frames_ref[...])
    live = jnp.sum(jnp.where(hit & (valid_ref[...] > 0), 1.0, 0.0), axis=1, keepdims=True)
    first, second = placed[:peers], placed[peers:]
    out_ref[0] = first[:, :128].astype(bf16)
    out_ref[1] = second[:, :128].astype(bf16)
    out_ref[2] = jnp.concatenate([first[:, 128:], second[:, 128:]], axis=1).astype(bf16)
    shard = jnp.concatenate([vw_ref[...].astype(f32), gw_ref[...].astype(f32)], axis=1)

    def lines(units):
        picked = [shard[3 * q + u // 3 : 3 * q + u // 3 + 1, 128 * (u % 3) : 128 * (u % 3) + 128] for q, u in units]
        return jnp.concatenate([jnp.concatenate(picked, axis=0)] * (peers // 8), axis=0)

    for k in range(4):
        out_ref[3 + k] = lines([(n // 2, 4 * (n % 2) + k) for n in range(8)]).astype(bf16)
    last = lines([(n // 2, 8) for n in range(8)])
    core = lax.broadcasted_iota(i32, (peers, 128), 0) % 2
    lane = lax.broadcasted_iota(i32, (peers, 128), 1)
    flag = lane - 64 * (1 - core)
    flags = jnp.where(flag == 0, live[:peers], 0.0) + jnp.where(flag == 1, live[peers:], 0.0)
    out_ref[7] = jnp.where(lane // 64 == core, last, flags).astype(bf16)


def turn_kernel(own_ref, rows_ref, out_ref, live_ref):
    width, slots = out_ref.shape
    peers = slots // 2
    channel = row_order(lax.broadcasted_iota(i32, (width, 128), 0))
    lane = lax.broadcasted_iota(i32, (width, 128), 1)
    low = (lane == channel).astype(bf16)
    at = lax.broadcasted_iota(i32, (16, 128), 1)
    for c in range(2):
        high = (lane == channel - 128 + 64 * c).astype(bf16)
        high = jnp.where((channel >= 128), high.astype(f32), 0.0).astype(bf16)
        turned = nt(low, rows_ref[c]) + nt(high, rows_ref[2])
        out_ref[:, c * peers : (c + 1) * peers] = turned.astype(bf16)
        flag = (at == 64 * (1 - own_ref[1]) + c).astype(bf16)
        live_ref[:, c * peers : (c + 1) * peers] = nt(flag, rows_ref[7])[:8]


def block_of(own_ref, k, blocks):
    n = blocks // 2
    x, y = own_ref[0] // 2, own_ref[0] % 2
    return ((x + n - k // 2) % n) * 2 + (y + k) % 2


def norm_kernel(own_ref, live_ref, gain_ref, *refs):
    normed_ref = refs[-1]
    blocks, width, slots = normed_ref.shape
    total = blocks * width
    live = live_ref[0:1, :]

    def block(k):
        return refs[k // 2][k % 2].astype(f32)

    s = jnp.zeros((1, slots), f32)
    for k in range(blocks):
        s = s + jnp.sum(block(k), axis=0, keepdims=True)
    mean = s * (1.0 / total)
    s = jnp.zeros((1, slots), f32)
    for k in range(blocks):
        c = block(k) - mean
        s = s + jnp.sum(c * c, axis=0, keepdims=True)
    inv = lax.rsqrt(s * (1.0 / total) + epsilon)
    for k in range(blocks):
        c = block(k) - mean
        normed_ref[k] = (c * inv * gain_ref[block_of(own_ref, k, blocks)] * live).astype(bf16)


def forward_kernel(own_ref, normed_ref, live_ref, wa_ref, wb_ref, up_ref, gated_ref, da_ref, db_ref, delta_ref, w_ref):
    blocks, width, slots = normed_ref.shape
    peers = slots // 2
    live = live_ref[0:1, :]
    first = own_ref[1] == 0
    lane = lax.broadcasted_iota(i32, (16, 128), 1)

    def unit(q, u, m):
        at = pl.ds(pl.multiple_of(16 * m, 16), 16)
        a, b = wa_ref[q, u % 4 if u < 8 else 4, at, :], wb_ref[q, u % 4 if u < 8 else 4, at, :]
        if u < 4:
            return jnp.where(first, a, b)
        if u < 8:
            return jnp.where(first, b, a)
        low, high = jnp.where(first, a, b).astype(f32), jnp.where(first, b, a).astype(f32)
        return jnp.where(lane < 64, low, high).astype(bf16)

    acc = jnp.zeros((2 * width, slots), f32)
    for k in range(blocks):
        m = block_of(own_ref, k, blocks)
        for q in range(4):
            for r in range(3):
                row = 48 * q + 16 * r
                w_ref[k, row : row + 16, :] = jnp.concatenate([unit(q, 3 * r + i, m) for i in range(3)], axis=1)
        acc = acc + tn(w_ref[k], normed_ref[k])
    value, gate = acc[:width], acc[width:]
    sig = jax.nn.sigmoid(gate)
    up = jnp.concatenate([up_ref[0], up_ref[1]], axis=1).astype(f32)
    gated = (value * sig).astype(bf16)
    gated_ref[0] = gated[:, :peers]
    gated_ref[1] = gated[:, peers:]
    value_delta = (up * sig * live).astype(bf16)
    gate_delta = (up * value * sig * (1.0 - sig) * live).astype(bf16)
    delta = jnp.concatenate([value_delta, gate_delta], axis=0)
    delta_ref[...] = delta
    target = owner_order(lax.broadcasted_iota(i32, (width, width), 0), own_ref[1])
    move = (target == row_order(lax.broadcasted_iota(i32, (width, width), 1))).astype(bf16)
    for k in range(blocks):
        dw = nt(nn(move, normed_ref[k]).astype(bf16), delta)
        m = block_of(own_ref, k, blocks)
        for j in range(4):
            da_ref[j, m] = dw[24 * j : 24 * j + 24].astype(bf16)
            db_ref[j, m] = dw[24 * j + 96 : 24 * j + 120].astype(bf16)


def backward_kernel(w_ref, delta_ref, *partial_refs):
    blocks = 2 * len(partial_refs)
    for k in range(blocks):
        partial_refs[k // 2][k % 2] = nn(w_ref[k], delta_ref[...]).astype(bf16)


def join_kernel(*refs):
    across_ref, out_ref = refs[-2:]
    width, slots = across_ref.shape[1:]
    peers = slots // 2
    s = jnp.zeros((width, slots), f32)
    for k, ref in enumerate(refs[:-2]):
        s = s + ref[0].astype(f32) + across_ref[k].astype(f32)
    place = lax.broadcasted_iota(i32, (width, width), 1)
    natural = lax.broadcasted_iota(i32, (width, width), 0)
    back = (row_order(place) == natural).astype(bf16)
    out = nn(back, s.astype(bf16)).astype(bf16)
    out_ref[0] = out[:, :peers]
    out_ref[1] = out[:, peers:]


def spread(x, axis, count):
    return lax.all_to_all(jnp.broadcast_to(x[None], (count,) + x.shape), axis, 0, 0, tiled=True)


def hop(x, step):
    n = lax.axis_size("x")
    return lax.ppermute(x, "x", [(i, (i + step) % n) for i in range(n)])


def swap(x, axis):
    return lax.ppermute(x, axis, [(0, 1), (1, 0)])


def stay(x):
    return x if INTERPRET else pltpu.with_memory_space_constraint(x, pltpu.HBM)


def body(frames, frame_owner, frame_valid, norm_gain, value_weight, gate_weight, grad_owned):
    far = lax.axis_size("zh")
    blocks = lax.axis_size(MP)
    peers = 8 * far
    slots = 2 * peers
    rows, width = frames.shape
    group = value_weight.shape[0]
    columns = 2 * width
    wt = columns // 128 * group // 4
    core = lax.axis_index("co").astype(i32)
    own = jnp.stack([lax.axis_index(MP).astype(i32), core])

    (sent,) = call(
        send_kernel,
        [((8, peers, 128), bf16)],
        *map(stay, (frames, frame_owner.reshape(1, rows), frame_valid.reshape(1, rows), value_weight, gate_weight)),
        scratch=[
            pltpu.VMEM((rows, width), bf16),
            pltpu.VMEM((1, rows), i32),
            pltpu.VMEM((1, rows), i32),
            pltpu.VMEM((group, width), bf16),
            pltpu.VMEM((group, width), bf16),
            pltpu.SemaphoreType.DMA((5,)),
        ],
        away=True,
    )
    got = lax.all_to_all(sent.transpose(1, 0, 2), DP, 0, 0, tiled=True)
    got = got.transpose(1, 0, 2)
    w_own = spread(got[3:], NEAR, 4)
    w_other = swap(w_own, "co")
    turned, live = call(turn_kernel, [((width, slots), bf16), ((8, slots), f32)], own, got)
    pair = jnp.stack([turned, swap(turned, "yl")])
    whole = [pair] + [hop(pair, dx) for dx in range(1, blocks // 2)]
    gain = norm_gain.reshape(blocks, 16, 4, 3).transpose(0, 2, 3, 1).reshape(blocks, width, 1)
    (normed,) = call(norm_kernel, [((blocks, width, slots), bf16)], own, live, gain, *whole)
    up = grad_owned.reshape(peers, 2, width).transpose(1, 2, 0)
    near = (4, blocks, 2 * group, columns)
    gated, dw_own, dw_other, delta, w_all = call(
        forward_kernel,
        [((2, width, peers), bf16), (near, bf16), (near, bf16), ((columns, slots), bf16), ((blocks, width, columns), bf16)],
        own,
        normed,
        live,
        w_own,
        w_other,
        up,
    )
    dw_c = swap(dw_other.reshape(4, far * group, columns), "co")
    partial = call(backward_kernel, [((2, width, slots), bf16)] * (blocks // 2), w_all, delta)
    dw_c = (dw_c.astype(f32) + dw_own.reshape(4, far * group, columns).astype(f32)).astype(bf16)
    dw_y = lax.all_to_all(dw_c, NEAR, 0, 0, tiled=True)
    dw_y = jnp.sum(dw_y.astype(f32), axis=0).astype(bf16)
    dw_y = dw_y.reshape(far, group, columns // 128, 128).transpose(0, 2, 1, 3).reshape(far, wt, 4, 128)
    dw_z = lax.all_to_all(dw_y, "zh", 0, 0, tiled=True)
    parts = [partial[0]] + [hop(partial[dx], -dx) for dx in range(1, blocks // 2)]
    other = []
    for part in parts:
        other.append(part[1:])
    across = swap(jnp.concatenate(other), "yl")
    (normed_grad,) = call(join_kernel, [((2, width, peers), bf16)], *parts, across)
    scale = float(rows * peers) ** (-0.5)
    grads = jnp.sum(dw_z.astype(f32), axis=0) * scale
    grads = grads.reshape(columns // 128, group, 128).transpose(1, 0, 2).reshape(group, columns)

    def restore(x):
        return x.transpose(2, 0, 1).reshape(1, peers, 2, width)

    return (restore(gated), grads[:, :width], grads[:, width:], restore(normed_grad))


def solution(mesh):
    mp = mesh.shape["mp"]
    far = mesh.shape["dp"] // 8
    fine = Mesh(mesh.devices.reshape(far, 2, 2, 2, mp // 2, 2), DP + MP)
    slots = P(DP, None, None, MP)
    weights = P(DP, MP)
    return jax.shard_map(
        body,
        mesh=fine,
        in_specs=(P(DP, MP), P(DP, None), P(DP), P(), weights, weights, slots),
        out_specs=(slots, weights, weights, slots),
        check_vma=False,
    )
```

```python
import jax
import jax.numpy as jnp
from jax import lax
from jax.experimental import pallas as pl
from jax.experimental.pallas import tpu as pltpu
from jax.sharding import Mesh, PartitionSpec as P


epsilon = 1e-05
bf16, f32, i32 = jnp.bfloat16, jnp.float32, jnp.int32
NEAR = ("zl", "yh")
DP = ("zh", "zl", "yh", "co")
MP = ("x", "yl")
INTERPRET = False


def nt(a, b):
    return lax.dot_general(a, b, (((1,), (1,)), ((), ())), preferred_element_type=f32)


def nn(a, b):
    return lax.dot_general(a, b, (((1,), (0,)), ((), ())), preferred_element_type=f32)


def tn(a, b):
    return lax.dot_general(a, b, (((0,), (0,)), ((), ())), preferred_element_type=f32)


def call(kernel, outs, *args, limit=12, scratch=(), away=False):
    vmem = pl.BlockSpec(memory_space=pltpu.VMEM)
    smem = pl.BlockSpec(memory_space=pltpu.SMEM)
    return pl.pallas_call(
        kernel,
        in_specs=[pl.BlockSpec(memory_space=pltpu.HBM) if away else smem if a.shape == (2,) else vmem for a in args],
        out_specs=[vmem] * len(outs),
        out_shape=[jax.ShapeDtypeStruct(s, d) for s, d in outs],
        scratch_shapes=list(scratch),
        compiler_params=pltpu.CompilerParams(vmem_limit_bytes=limit << 20),
        interpret=INTERPRET,
    )(*args)


def row_order(p):
    return (p % 16) * 12 + (p // 48) * 3 + (p // 16) % 3


def owner_order(p, co):
    core = (p // 96 + co) % 2
    return ((p // 12) % 2) * 96 + (((p // 24) % 4) * 2 + core) * 12 + p % 12


def send_kernel(frames_hbm, owner_hbm, valid_hbm, vw_hbm, gw_hbm, out_ref, frames_ref, owner_ref, valid_ref, vw_ref, gw_ref, sems):
    pairs = ((owner_hbm, owner_ref), (valid_hbm, valid_ref), (frames_hbm, frames_ref), (vw_hbm, vw_ref), (gw_hbm, gw_ref))
    copies = [pltpu.make_async_copy(a, b, sems.at[i]) for i, (a, b) in enumerate(pairs)]
    for copy in copies:
        copy.start()
    for copy in copies:
        copy.wait()
    rows, _ = frames_ref.shape
    peers = out_ref.shape[1]
    owner = owner_ref[...]
    down = jnp.transpose(jnp.broadcast_to(owner, (rows, rows)))
    earlier = lax.broadcasted_iota(i32, (rows, rows), 0) < lax.broadcasted_iota(i32, (rows, rows), 1)
    slot = jnp.sum(jnp.where((down == owner) & earlier, 1.0, 0.0), axis=0, keepdims=True).astype(i32)
    hit = lax.broadcasted_iota(i32, (2 * peers, rows), 0) == slot * peers + owner
    placed = nn(jnp.where(hit, 1.0, 0.0).astype(bf16), frames_ref[...])
    live = jnp.sum(jnp.where(hit & (valid_ref[...] > 0), 1.0, 0.0), axis=1, keepdims=True)
    first, second = placed[:peers], placed[peers:]
    out_ref[0] = first[:, :128].astype(bf16)
    out_ref[1] = second[:, :128].astype(bf16)
    out_ref[2] = jnp.concatenate([first[:, 128:], second[:, 128:]], axis=1).astype(bf16)
    shard = jnp.concatenate([vw_ref[...].astype(f32), gw_ref[...].astype(f32)], axis=1)

    def lines(units):
        picked = [shard[3 * q + u // 3 : 3 * q + u // 3 + 1, 128 * (u % 3) : 128 * (u % 3) + 128] for q, u in units]
        return jnp.concatenate([jnp.concatenate(picked, axis=0)] * (peers // 8), axis=0)

    for k in range(4):
        out_ref[3 + k] = lines([(n // 2, 4 * (n % 2) + k) for n in range(8)]).astype(bf16)
    last = lines([(n // 2, 8) for n in range(8)])
    core = lax.broadcasted_iota(i32, (peers, 128), 0) % 2
    lane = lax.broadcasted_iota(i32, (peers, 128), 1)
    flag = lane - 64 * (1 - core)
    flags = jnp.where(flag == 0, live[:peers], 0.0) + jnp.where(flag == 1, live[peers:], 0.0)
    out_ref[7] = jnp.where(lane // 64 == core, last, flags).astype(bf16)


def turn_kernel(own_ref, rows_ref, out_ref, live_ref):
    width, slots = out_ref.shape
    peers = slots // 2
    channel = row_order(lax.broadcasted_iota(i32, (width, 128), 0))
    lane = lax.broadcasted_iota(i32, (width, 128), 1)
    low = (lane == channel).astype(bf16)
    at = lax.broadcasted_iota(i32, (16, 128), 1)
    for c in range(2):
        high = (lane == channel - 128 + 64 * c).astype(bf16)
        high = jnp.where((channel >= 128), high.astype(f32), 0.0).astype(bf16)
        turned = nt(low, rows_ref[c]) + nt(high, rows_ref[2])
        out_ref[:, c * peers : (c + 1) * peers] = turned.astype(bf16)
        flag = (at == 64 * (1 - own_ref[1]) + c).astype(bf16)
        live_ref[:, c * peers : (c + 1) * peers] = nt(flag, rows_ref[7])[:8]


def block_of(own_ref, k, blocks):
    n = blocks // 2
    x, y = own_ref[0] // 2, own_ref[0] % 2
    return ((x + n - k // 2) % n) * 2 + (y + k) % 2


def norm_kernel(own_ref, live_ref, gain_ref, *refs):
    normed_ref = refs[-1]
    blocks, width, slots = normed_ref.shape
    total = blocks * width
    live = live_ref[0:1, :]

    def block(k):
        return refs[k // 2][k % 2].astype(f32)

    s = jnp.zeros((1, slots), f32)
    for k in range(blocks):
        s = s + jnp.sum(block(k), axis=0, keepdims=True)
    mean = s * (1.0 / total)
    s = jnp.zeros((1, slots), f32)
    for k in range(blocks):
        c = block(k) - mean
        s = s + jnp.sum(c * c, axis=0, keepdims=True)
    inv = lax.rsqrt(s * (1.0 / total) + epsilon)
    for k in range(blocks):
        c = block(k) - mean
        normed_ref[k] = (c * inv * gain_ref[block_of(own_ref, k, blocks)] * live).astype(bf16)


def forward_kernel(own_ref, normed_ref, live_ref, wa_ref, wb_ref, up_ref, gated_ref, db_ref, delta_ref, w_ref):
    blocks, width, slots = normed_ref.shape
    peers = slots // 2
    live = live_ref[0:1, :]
    first = own_ref[1] == 0
    lane = lax.broadcasted_iota(i32, (16, 128), 1)

    def unit(q, u, m):
        at = pl.ds(pl.multiple_of(16 * m, 16), 16)
        a, b = wa_ref[q, u % 4 if u < 8 else 4, at, :], wb_ref[q, u % 4 if u < 8 else 4, at, :]
        if u < 4:
            return jnp.where(first, a, b)
        if u < 8:
            return jnp.where(first, b, a)
        low, high = jnp.where(first, a, b).astype(f32), jnp.where(first, b, a).astype(f32)
        return jnp.where(lane < 64, low, high).astype(bf16)

    acc = jnp.zeros((2 * width, slots), f32)
    for k in range(blocks):
        m = block_of(own_ref, k, blocks)
        for q in range(4):
            for r in range(3):
                row = 48 * q + 16 * r
                w_ref[k, row : row + 16, :] = jnp.concatenate([unit(q, 3 * r + i, m) for i in range(3)], axis=1)
        acc = acc + tn(w_ref[k], normed_ref[k])
    value, gate = acc[:width], acc[width:]
    sig = jax.nn.sigmoid(gate)
    up = jnp.concatenate([up_ref[0], up_ref[1]], axis=1).astype(f32)
    gated = (value * sig).astype(bf16)
    gated_ref[0] = gated[:, :peers]
    gated_ref[1] = gated[:, peers:]
    value_delta = (up * sig * live).astype(bf16)
    gate_delta = (up * value * sig * (1.0 - sig) * live).astype(bf16)
    delta = jnp.concatenate([value_delta, gate_delta], axis=0)
    delta_ref[...] = delta
    owner_rows(own_ref, normed_ref, delta, db_ref, 96)


def owner_rows(own_ref, normed_ref, delta, out_ref, start):
    blocks, width, _ = normed_ref.shape
    target = owner_order(lax.broadcasted_iota(i32, (96, width), 0) + start, own_ref[1])
    move = (target == row_order(lax.broadcasted_iota(i32, (96, width), 1))).astype(bf16)
    for k in range(blocks):
        dw = nt(nn(move, normed_ref[k]).astype(bf16), delta)
        m = block_of(own_ref, k, blocks)
        for j in range(4):
            out_ref[j, m] = dw[24 * j : 24 * j + 24].astype(bf16)


def own_rows_kernel(own_ref, normed_ref, delta_ref, da_ref):
    owner_rows(own_ref, normed_ref, delta_ref[...], da_ref, 0)


def backward_kernel(w_ref, delta_ref, *partial_refs):
    blocks = 2 * len(partial_refs)
    for k in range(blocks):
        partial_refs[k // 2][k % 2] = nn(w_ref[k], delta_ref[...]).astype(bf16)


def join_kernel(*refs):
    across_ref, out_ref = refs[-2:]
    width, slots = across_ref.shape[1:]
    peers = slots // 2
    s = jnp.zeros((width, slots), f32)
    for k, ref in enumerate(refs[:-2]):
        s = s + ref[0].astype(f32) + across_ref[k].astype(f32)
    place = lax.broadcasted_iota(i32, (width, width), 1)
    natural = lax.broadcasted_iota(i32, (width, width), 0)
    back = (row_order(place) == natural).astype(bf16)
    out = nn(back, s.astype(bf16)).astype(bf16)
    out_ref[0] = out[:, :peers]
    out_ref[1] = out[:, peers:]


def spread(x, axis, count):
    return lax.all_to_all(jnp.broadcast_to(x[None], (count,) + x.shape), axis, 0, 0, tiled=True)


def hop(x, step):
    n = lax.axis_size("x")
    return lax.ppermute(x, "x", [(i, (i + step) % n) for i in range(n)])


def swap(x, axis):
    return lax.ppermute(x, axis, [(0, 1), (1, 0)])


def stay(x):
    return x if INTERPRET else pltpu.with_memory_space_constraint(x, pltpu.HBM)


def body(frames, frame_owner, frame_valid, norm_gain, value_weight, gate_weight, grad_owned):
    far = lax.axis_size("zh")
    blocks = lax.axis_size(MP)
    peers = 8 * far
    slots = 2 * peers
    rows, width = frames.shape
    group = value_weight.shape[0]
    columns = 2 * width
    wt = columns // 128 * group // 4
    core = lax.axis_index("co").astype(i32)
    own = jnp.stack([lax.axis_index(MP).astype(i32), core])

    (sent,) = call(
        send_kernel,
        [((8, peers, 128), bf16)],
        *map(stay, (frames, frame_owner.reshape(1, rows), frame_valid.reshape(1, rows), value_weight, gate_weight)),
        scratch=[
            pltpu.VMEM((rows, width), bf16),
            pltpu.VMEM((1, rows), i32),
            pltpu.VMEM((1, rows), i32),
            pltpu.VMEM((group, width), bf16),
            pltpu.VMEM((group, width), bf16),
            pltpu.SemaphoreType.DMA((5,)),
        ],
        away=True,
    )
    got = lax.all_to_all(sent.transpose(1, 0, 2), DP, 0, 0, tiled=True)
    got = got.transpose(1, 0, 2)
    w_own = spread(got[3:], NEAR, 4)
    w_other = swap(w_own, "co")
    turned, live = call(turn_kernel, [((width, slots), bf16), ((8, slots), f32)], own, got)
    pair = jnp.stack([turned, swap(turned, "yl")])
    whole = [pair] + [hop(pair, dx) for dx in range(1, blocks // 2)]
    gain = norm_gain.reshape(blocks, 16, 4, 3).transpose(0, 2, 3, 1).reshape(blocks, width, 1)
    (normed,) = call(norm_kernel, [((blocks, width, slots), bf16)], own, live, gain, *whole)
    up = grad_owned.reshape(peers, 2, width).transpose(1, 2, 0)
    near = (4, blocks, 2 * group, columns)
    gated, dw_other, delta, w_all = call(
        forward_kernel,
        [((2, width, peers), bf16), (near, bf16), ((columns, slots), bf16), ((blocks, width, columns), bf16)],
        own,
        normed,
        live,
        w_own,
        w_other,
        up,
    )
    dw_c = swap(dw_other.reshape(4, far * group, columns), "co")
    (dw_own,) = call(own_rows_kernel, [(near, bf16)], own, normed, delta)
    partial = call(backward_kernel, [((2, width, slots), bf16)] * (blocks // 2), w_all, delta)
    dw_c = (dw_c.astype(f32) + dw_own.reshape(4, far * group, columns).astype(f32)).astype(bf16)
    dw_y = lax.all_to_all(dw_c, NEAR, 0, 0, tiled=True)
    dw_y = jnp.sum(dw_y.astype(f32), axis=0).astype(bf16)
    dw_y = dw_y.reshape(far, group, columns // 128, 128).transpose(0, 2, 1, 3).reshape(far, wt, 4, 128)
    dw_z = lax.all_to_all(dw_y, "zh", 0, 0, tiled=True)
    parts = [partial[0]] + [hop(partial[dx], -dx) for dx in range(1, blocks // 2)]
    other = []
    for part in parts:
        other.append(part[1:])
    across = swap(jnp.concatenate(other), "yl")
    (normed_grad,) = call(join_kernel, [((2, width, peers), bf16)], *parts, across)
    scale = float(rows * peers) ** (-0.5)
    grads = jnp.sum(dw_z.astype(f32), axis=0) * scale
    grads = grads.reshape(columns // 128, group, 128).transpose(1, 0, 2).reshape(group, columns)

    def restore(x):
        return x.transpose(2, 0, 1).reshape(1, peers, 2, width)

    return (restore(gated), grads[:, :width], grads[:, width:], restore(normed_grad))


def solution(mesh):
    mp = mesh.shape["mp"]
    far = mesh.shape["dp"] // 8
    fine = Mesh(mesh.devices.reshape(far, 2, 2, 2, mp // 2, 2), DP + MP)
    slots = P(DP, None, None, MP)
    weights = P(DP, MP)
    return jax.shard_map(
        body,
        mesh=fine,
        in_specs=(P(DP, MP), P(DP, None), P(DP), P(), weights, weights, slots),
        out_specs=(slots, weights, weights, slots),
        check_vma=False,
    )
```
